512 devices in a mesh: row: 16 (over z_lo, y), col: 32 (over x, z_hi, core).
Axes of the slice: x: 4, y: 4, z: 16 (z_hi: 4, z_lo: 4; z = z_hi * 4 + z_lo), core: 2. Of those that a mesh axis runs over, the one named last changes fastest.
Arguments:
- features: bfloat16 [8, 2048, 768], P(None, 'row', 'col'), may hold values from -6 to 6
- lengthscale: float32 [768], replicated, may hold values from 8 to 200
- noise: float32 [8, 2048], P(None, 'row'), may hold values from 0.05 to 0.5
Outputs:
- panel: float32 [8, 2048, 128], P(None, 'row')
- trailing: float32 [8, 2048, 4, 4096], P(None, 'row', None, 'col')
The draws below stay inside these ranges and needn't reach their ends.
All inputs are finite; a program needn't handle non-finite values.
Results may differ from the reference program's by a relative error of at most 0.005.
Values may be sent and summed in bfloat16 or wider, within the bound.
A program may use at most 64 MiB of HBM per device.

```python
import math
import jax
import jax.numpy as jnp
from jax import lax

D = 768
B = 128
TR = 8
N_ROW = 16
N_COL = 32


def block_levels(own_key, shape, cuts, least, high):
    level, own = 1.0, jax.random.fold_in(own_key, 6)
    for dim, shards_of in cuts:
        heights = jnp.exp(jax.random.uniform(jax.random.fold_in(own, dim), (shards_of,), jnp.float32, least / len(cuts), high / len(cuts)))
        level = level * jnp.repeat(heights, shape[dim] // shards_of).reshape([-1 if axis == dim else 1 for axis in range(len(shape))])
    return level


def scatter_about(own_key, dims, scale, most, shards=(), dtype=jnp.bfloat16):
    entries = jax.random.normal(own_key, dims, jnp.float32) * scale
    if len(shards) > 0:
        entries = block_levels(own_key, dims, shards, -0.22, 0.18) * entries
    return jnp.clip(entries, min=-most, max=most).astype(dtype)


def setup_inputs(seed: int = 0) -> dict:
    splits = jax.random.split(jax.random.key(seed), 4)
    return {
        "features": scatter_about(splits[0], (TR, N_ROW * B, D), 1.0, 6.0, ((1, 16), (2, 32))),
        "lengthscale": jnp.clip(jnp.exp(jax.random.uniform(splits[1], (D,), jnp.float32, math.log(8.0), math.log(200.0))), 8.0, 200.0),
        "noise": jnp.clip(jnp.exp(math.log(0.5) - 2.3025851 * jax.random.uniform(splits[2], (TR, N_ROW * B), jnp.float32) ** block_levels(splits[2], (TR, N_ROW * B), ((1, 16),), -0.2, 0.2)), 0.05, 0.5),
    }


def reference(features, lengthscale, noise):
    npts = features.shape[0] * features.shape[1]
    scaled = features.reshape(npts, features.shape[2]).astype(jnp.float32) / lengthscale[None, :]
    sq = jnp.sum(scaled * scaled, axis=1)
    gram = jnp.dot(scaled, scaled.T, precision=lax.Precision.HIGHEST)
    kern = jnp.exp(-0.5 * (sq[:, None] + sq[None, :] - 2.0 * gram))
    index = jnp.arange(npts)
    kern = kern.at[index, index].add(noise.reshape(npts))
    width = B
    factor = jnp.linalg.cholesky(kern[:width, :width])
    panel = jax.scipy.linalg.solve_triangular(factor, kern[:, :width].T, lower=True).T
    trailing = kern - jnp.dot(panel, panel.T, precision=lax.Precision.HIGHEST)
    rows = features.shape[1]
    tiles_col = npts // (N_COL * width)
    return (panel.reshape(features.shape[0], rows, width), trailing.reshape(features.shape[0], rows, tiles_col, N_COL * width))
```

```python
import jax
import jax.numpy as jnp
from jax import lax
from jax.experimental import pallas as pl
from jax.experimental.pallas import tpu as pltpu
from jax.sharding import PartitionSpec as P

MESH = pl.DeviceIdType.MESH
NCH = 4


def rcopy(src, dst, ss, rs, dev):
    return pltpu.make_async_remote_copy(
        src_ref=src, dst_ref=dst, send_sem=ss, recv_sem=rs, device_id=dev, device_id_type=MESH
    )


def place():
    r = lax.axis_index("row")
    c = lax.axis_index("col")
    return (
        lax.div(r, 4),
        lax.rem(r, 4),
        lax.div(c, 8),
        lax.rem(lax.div(c, 2), 4),
        lax.rem(c, 2),
    )


def dev(zl, y, x, zh, core):
    return (zl * 4 + y, (x * 4 + zh) * 2 + core)


def comm_kernel(
    f_ref, n_ref, rows, cols, t0, nz,
    s1s, s1r, loc, s2s, s2r, s3s, s3r, tcs_, tcr, tts, ttr, cl,
):
    zl, y, x, zh, core = place()
    oc = 1 - core
    zp, zm = lax.rem(zh + 1, 4), lax.rem(zh + 3, 4)
    xp, xm, xo = lax.rem(x + 1, 4), lax.rem(x + 3, 4), lax.rem(x + 2, 4)
    yp, ym = lax.rem(y + 1, 4), lax.rem(y + 3, 4)
    lp, lm = lax.rem(zl + 1, 4), lax.rem(zl + 3, 4)
    d_zp, d_zm = dev(zl, y, x, zp, core), dev(zl, y, x, zm, core)
    d_xp, d_xm = dev(zl, y, xp, zh, core), dev(zl, y, xm, zh, core)
    d_co = dev(zl, y, x, zh, oc)
    d_yp, d_ym = dev(zl, yp, x, zh, core), dev(zl, ym, x, zh, core)
    d_lp, d_lm = dev(lp, y, x, zh, core), dev(lm, y, x, zh, core)
    partners = (d_zp, d_zm, d_xp, d_xm, d_co, d_yp, d_ym, d_lp, d_lm)
    bar = pltpu.get_barrier_semaphore()
    for d in partners:
        pl.semaphore_signal(bar, inc=1, device_id=d, device_id_type=MESH)
    pl.semaphore_wait(bar, len(partners))

    def zrow(zz):
        return pl.multiple_of(((core * 4 + x) * 4 + zz) * 24, 8)

    def xrow(kk, xx):
        return pl.multiple_of((kk * 4 + xx) * 96, 32)

    own = rows.at[:, :, pl.ds(zrow(zh), 24), :]
    up = rcopy(f_ref, own, s1s.at[0], s1r.at[0], d_zp)
    dn = rcopy(f_ref, own, s1s.at[1], s1r.at[1], d_zm)
    up.start()
    dn.start()
    me = pltpu.make_async_copy(f_ref, own, loc)
    me.start()
    from_m = rows.at[:, :, pl.ds(zrow(zm), 24), :]
    from_p = rows.at[:, :, pl.ds(zrow(zp), 24), :]
    rcopy(from_m, from_m, s1s.at[0], s1r.at[0], d_zp).wait_recv()
    a = rows.at[:, 0, pl.ds(zrow(zm), 24), :]
    fa = rcopy(a, a, s1s.at[2], s1r.at[2], d_zp)
    fa.start()
    rcopy(from_p, from_p, s1s.at[1], s1r.at[1], d_zm).wait_recv()
    b = rows.at[:, 1, pl.ds(zrow(zp), 24), :]
    fb = rcopy(b, b, s1s.at[3], s1r.at[3], d_zm)
    fb.start()
    zo = lax.rem(zh + 2, 4)
    oa = rows.at[:, 0, pl.ds(zrow(zo), 24), :]
    ob = rows.at[:, 1, pl.ds(zrow(zo), 24), :]
    rcopy(oa, oa, s1s.at[2], s1r.at[2], d_zp).wait_recv()
    rcopy(ob, ob, s1s.at[3], s1r.at[3], d_zm).wait_recv()
    me.wait()
    sends = [up, dn, fa, fb]

    def blk(kk, xx, par):
        return rows.at[:, par, pl.ds(xrow(kk, xx), 96), :]

    for par in range(2):
        o = blk(core, x, par)
        for i, d in enumerate((d_xp, d_xm, d_co)):
            cp = rcopy(o, o, s2s.at[par, i], s2r.at[par, i], d)
            cp.start()
            sends.append(cp)
    for par in range(2):
        m = blk(core, xm, par)
        rcopy(m, m, s2s.at[par, 0], s2r.at[par, 0], d_xp).wait_recv()
        if par == 0:
            cp = rcopy(m, m, s2s.at[par, 3], s2r.at[par, 3], d_xp)
            cp.start()
            sends.append(cp)
        cp = rcopy(m, m, s2s.at[par, 4], s2r.at[par, 4], d_co)
        cp.start()
        sends.append(cp)
        p = blk(core, xp, par)
        rcopy(p, p, s2s.at[par, 1], s2r.at[par, 1], d_xm).wait_recv()
        if par == 1:
            cp = rcopy(p, p, s2s.at[par, 3], s2r.at[par, 3], d_xm)
            cp.start()
            sends.append(cp)
        cp = rcopy(p, p, s2s.at[par, 5], s2r.at[par, 5], d_co)
        cp.start()
        sends.append(cp)
    for par in range(2):
        o = blk(core, xo, par)
        rcopy(o, o, s2s.at[par, 3], s2r.at[par, 3], d_xp).wait_recv()
        cp = rcopy(o, o, s2s.at[par, 6], s2r.at[par, 6], d_co)
        cp.start()
        sends.append(cp)
    for par in range(2):
        for xx, i in ((x, 2), (xm, 4), (xp, 5), (xo, 6)):
            o = blk(oc, xx, par)
            rcopy(o, o, s2s.at[par, i], s2r.at[par, i], d_co).wait_recv()

    turn = 1 - 2 * core
    y_a = lax.rem(y + turn + 4, 4)
    y_b = lax.rem(y - turn + 4, 4)
    d_a, d_b = dev(zl, y_a, x, zh, core), dev(zl, y_b, x, zh, core)

    def tree(zr, yr, chunks, srcs, send, recv, lsem):
        on = y == yr
        root = jnp.logical_and(on, zl == zr)
        off = jnp.logical_not(root)
        c_up = jnp.logical_and(on, jnp.logical_and(zl >= zr, zl < 3))
        c_dn = jnp.logical_and(on, jnp.logical_and(zl <= zr, zl > 0))
        c_b = jnp.logical_or(on, y == lax.rem(yr - turn + 4, 4))
        outs = ((c_up, d_lp), (c_dn, d_lm), (on, d_a), (c_b, d_b))
        for k, ch in enumerate(chunks):
            @pl.when(root)
            def _():
                cp = pltpu.make_async_copy(srcs[k], ch, lsem.at[k])
                cp.start()
                cp.wait()

            @pl.when(off)
            def _():
                rcopy(ch, ch, send.at[k, 0], recv.at[k], d_lp).wait_recv()

            for i, (cond, d) in enumerate(outs):
                @pl.when(cond)
                def _():
                    rcopy(ch, ch, send.at[k, i], recv.at[k], d).start()

        def finish():
            for k, ch in enumerate(chunks):
                for i, (cond, d) in enumerate(outs):
                    @pl.when(cond)
                    def _():
                        rcopy(ch, ch, send.at[k, i], recv.at[k], d).wait_send()

        return finish

    f0 = tree(0, 0, [t0, nz], [rows.at[0, 0], n_ref], tts, ttr, cl.at[0])
    step = 768 // NCH
    par = lax.div(x, 2)
    f1 = tree(
        lax.rem(x, 2) * 2 + lax.div(zh, 2),
        lax.rem(zh, 2) * 2 + core,
        [cols.at[:, pl.ds(k * step, step), :] for k in range(NCH)],
        [rows.at[:, par, pl.ds(k * step, step), :] for k in range(NCH)],
        tcs_, tcr, cl.at[1],
    )
    f0()
    f1()
    for cp in sends:
        cp.wait_send()


def gather(f, noise):
    DMA = pltpu.SemaphoreType.DMA
    vm = pl.BlockSpec(memory_space=pltpu.VMEM)
    return pl.pallas_call(
        comm_kernel,
        out_shape=(
            jax.ShapeDtypeStruct((4, 2, 768, 128), jnp.bfloat16),
            jax.ShapeDtypeStruct((4, 768, 128), jnp.bfloat16),
            jax.ShapeDtypeStruct((768, 128), jnp.bfloat16),
            jax.ShapeDtypeStruct((8, 128), jnp.float32),
        ),
        in_specs=[vm, vm],
        out_specs=(vm, vm, vm, vm),
        scratch_shapes=[
            DMA((4,)), DMA((4,)), DMA,
            DMA((2, 7)), DMA((2, 7)), DMA((1,)), DMA((1,)),
            DMA((NCH, 4)), DMA((NCH,)),
            DMA((2, 4)), DMA((2,)), DMA((2, NCH)),
        ],
        compiler_params=pltpu.CompilerParams(collective_id=0, has_side_effects=True),
        name="gather_features",
    )(f, noise)


def body(features, lengthscale, noise):
    row_id = lax.axis_index("row")
    col_id = lax.axis_index("col")
    f = jnp.transpose(features, (0, 2, 1)).reshape(4, 2, 24, 128)
    rows, cols, t0, nz = gather(f, noise)
    ls = lengthscale.reshape(4, 4, 2, 24).transpose(2, 0, 1, 3).reshape(768)
    w = 1.0 / (ls * ls)
    A = rows.reshape(8, 768, 128).astype(jnp.float32)
    C = cols.astype(jnp.float32)
    T = t0.astype(jnp.float32)
    Cw = C * w[None, :, None]
    Tw = T * w[:, None]
    asq = jnp.sum(A * A * w[None, :, None], axis=1)
    csq = jnp.sum(C * Cw, axis=1)
    tsq = jnp.sum(T * Tw, axis=0)
    hi = lax.Precision.HIGHEST
    inner = jnp.arange(128, dtype=jnp.int32)
    eye = inner[:, None] == inner[None, :]
    n0 = noise[0]
    gt = jnp.einsum("kp,kq->pq", T, Tw, precision=hi)
    ga = jnp.einsum("tkp,kq->tpq", A, Tw, precision=hi)
    gc = jnp.einsum("tkp,kq->tpq", C, Tw, precision=hi)
    g = jnp.einsum("tkp,ukq->tpuq", A, Cw, precision=hi)
    noise0 = nz[0]
    k0 = jnp.exp(gt - 0.5 * (tsq[:, None] + tsq[None, :])) + jnp.where(eye, noise0[:, None], 0.0)
    factor = jnp.linalg.cholesky(k0)
    inv = jax.scipy.linalg.solve_triangular(factor, eye.astype(jnp.float32), lower=True)
    ka = jnp.exp(ga - 0.5 * (asq[:, :, None] + tsq[None, None, :]))
    first = (jnp.arange(8, dtype=jnp.int32) * 16 + row_id) == 0
    ka = ka + jnp.where(first[:, None, None] & eye[None], n0[None, :, None], 0.0)
    kc = jnp.exp(gc - 0.5 * (csq[:, :, None] + tsq[None, None, :]))
    first = (jnp.arange(4, dtype=jnp.int32) * 32 + col_id) == 0
    kc = kc + jnp.where(first[:, None, None] & eye[None], noise0[None, :, None], 0.0)
    pa = jnp.einsum("tpk,qk->tpq", ka, inv, precision=hi)
    pc = jnp.einsum("tpk,qk->tpq", kc, inv, precision=hi)
    k = jnp.exp(g - 0.5 * (asq[:, :, None, None] + csq[None, None, :, :]))
    tr = jnp.arange(8, dtype=jnp.int32) * 16 + row_id
    tc = jnp.arange(4, dtype=jnp.int32) * 32 + col_id
    same = tr[:, None, None, None] == tc[None, None, :, None]
    k = k + jnp.where(same & eye[None, :, None, :], noise[:, :, None, None], 0.0)
    return pa, k - jnp.einsum("tpk,uqk->tpuq", pa, pc, precision=hi)


def solution(mesh):
    placed = (P(None, "row", "col"), P(), P(None, "row"))
    return jax.shard_map(
        body,
        mesh=mesh,
        in_specs=placed,
        out_specs=(P(None, "row", None), P(None, "row", None, "col")),
        check_vma=False,
    )
```

```python
import jax
import jax.numpy as jnp
from jax import lax
from jax.experimental import pallas as pl
from jax.experimental.pallas import tpu as pltpu
from jax.sharding import PartitionSpec as P

MESH = pl.DeviceIdType.MESH
NCH = 4


def rcopy(src, dst, ss, rs, dev):
    return pltpu.make_async_remote_copy(
        src_ref=src, dst_ref=dst, send_sem=ss, recv_sem=rs, device_id=dev, device_id_type=MESH
    )


def place():
    r = lax.axis_index("row")
    c = lax.axis_index("col")
    return (
        lax.div(r, 4),
        lax.rem(r, 4),
        lax.div(c, 8),
        lax.rem(lax.div(c, 2), 4),
        lax.rem(c, 2),
    )


def dev(zl, y, x, zh, core):
    return (zl * 4 + y, (x * 4 + zh) * 2 + core)


def comm_kernel(
    f_ref, n_ref, rows, cols, t0, nz,
    s1s, s1r, loc, s2s, s2r, s3s, s3r, tcs_, tcr, tts, ttr, cl,
):
    zl, y, x, zh, core = place()
    oc = 1 - core
    zp, zm = lax.rem(zh + 1, 4), lax.rem(zh + 3, 4)
    xp, xm, xo = lax.rem(x + 1, 4), lax.rem(x + 3, 4), lax.rem(x + 2, 4)
    yp, ym = lax.rem(y + 1, 4), lax.rem(y + 3, 4)
    lp, lm = lax.rem(zl + 1, 4), lax.rem(zl + 3, 4)
    d_zp, d_zm = dev(zl, y, x, zp, core), dev(zl, y, x, zm, core)
    d_xp, d_xm = dev(zl, y, xp, zh, core), dev(zl, y, xm, zh, core)
    d_co = dev(zl, y, x, zh, oc)
    d_yp, d_ym = dev(zl, yp, x, zh, core), dev(zl, ym, x, zh, core)
    d_lp, d_lm = dev(lp, y, x, zh, core), dev(lm, y, x, zh, core)
    partners = (d_zp, d_zm, d_xp, d_xm, d_co, d_yp, d_ym, d_lp, d_lm)
    bar = pltpu.get_barrier_semaphore()
    for d in partners:
        pl.semaphore_signal(bar, inc=1, device_id=d, device_id_type=MESH)
    pl.semaphore_wait(bar, len(partners))

    def zrow(zz):
        return pl.multiple_of(((core * 4 + x) * 4 + zz) * 24, 8)

    def xrow(kk, xx):
        return pl.multiple_of((kk * 4 + xx) * 96, 32)

    own = rows.at[:, :, pl.ds(zrow(zh), 24), :]
    up = rcopy(f_ref, own, s1s.at[0], s1r.at[0], d_zp)
    dn = rcopy(f_ref, own, s1s.at[1], s1r.at[1], d_zm)
    up.start()
    dn.start()
    me = pltpu.make_async_copy(f_ref, own, loc)
    me.start()
    from_m = rows.at[:, :, pl.ds(zrow(zm), 24), :]
    from_p = rows.at[:, :, pl.ds(zrow(zp), 24), :]
    rcopy(from_m, from_m, s1s.at[0], s1r.at[0], d_zp).wait_recv()
    a = rows.at[:, 0, pl.ds(zrow(zm), 24), :]
    fa = rcopy(a, a, s1s.at[2], s1r.at[2], d_zp)
    fa.start()
    rcopy(from_p, from_p, s1s.at[1], s1r.at[1], d_zm).wait_recv()
    b = rows.at[:, 1, pl.ds(zrow(zp), 24), :]
    fb = rcopy(b, b, s1s.at[3], s1r.at[3], d_zm)
    fb.start()
    zo = lax.rem(zh + 2, 4)
    oa = rows.at[:, 0, pl.ds(zrow(zo), 24), :]
    ob = rows.at[:, 1, pl.ds(zrow(zo), 24), :]
    rcopy(oa, oa, s1s.at[2], s1r.at[2], d_zp).wait_recv()
    rcopy(ob, ob, s1s.at[3], s1r.at[3], d_zm).wait_recv()
    me.wait()
    sends = [up, dn, fa, fb]

    def blk(kk, xx, par):
        return rows.at[:, par, pl.ds(xrow(kk, xx), 96), :]

    for par in range(2):
        o = blk(core, x, par)
        for i, d in enumerate((d_xp, d_xm, d_co)):
            cp = rcopy(o, o, s2s.at[par, i], s2r.at[par, i], d)
            cp.start()
            sends.append(cp)
    for par in range(2):
        m = blk(core, xm, par)
        rcopy(m, m, s2s.at[par, 0], s2r.at[par, 0], d_xp).wait_recv()
        if par == 0:
            cp = rcopy(m, m, s2s.at[par, 3], s2r.at[par, 3], d_xp)
            cp.start()
            sends.append(cp)
        cp = rcopy(m, m, s2s.at[par, 4], s2r.at[par, 4], d_co)
        cp.start()
        sends.append(cp)
        p = blk(core, xp, par)
        rcopy(p, p, s2s.at[par, 1], s2r.at[par, 1], d_xm).wait_recv()
        if par == 1:
            cp = rcopy(p, p, s2s.at[par, 3], s2r.at[par, 3], d_xm)
            cp.start()
            sends.append(cp)
        cp = rcopy(p, p, s2s.at[par, 5], s2r.at[par, 5], d_co)
        cp.start()
        sends.append(cp)
    for par in range(2):
        o = blk(core, xo, par)
        rcopy(o, o, s2s.at[par, 3], s2r.at[par, 3], d_xp).wait_recv()
        cp = rcopy(o, o, s2s.at[par, 6], s2r.at[par, 6], d_co)
        cp.start()
        sends.append(cp)
    for par in range(2):
        for xx, i in ((x, 2), (xm, 4), (xp, 5), (xo, 6)):
            o = blk(oc, xx, par)
            rcopy(o, o, s2s.at[par, i], s2r.at[par, i], d_co).wait_recv()

    turn = 1 - 2 * core
    y_a = lax.rem(y + turn + 4, 4)
    y_b = lax.rem(y - turn + 4, 4)
    d_a, d_b = dev(zl, y_a, x, zh, core), dev(zl, y_b, x, zh, core)

    def tree(zr, yr, chunks, srcs, send, recv, lsem):
        on = y == yr
        root = jnp.logical_and(on, zl == zr)
        off = jnp.logical_not(root)
        c_up = jnp.logical_and(on, jnp.logical_and(zl >= zr, zl < 3))
        c_dn = jnp.logical_and(on, jnp.logical_and(zl <= zr, zl > 0))
        c_b = jnp.logical_or(on, y == lax.rem(yr - turn + 4, 4))
        outs = ((c_up, d_lp), (c_dn, d_lm), (on, d_a), (c_b, d_b))
        for k, ch in enumerate(chunks):
            @pl.when(root)
            def _():
                cp = pltpu.make_async_copy(srcs[k], ch, lsem.at[k])
                cp.start()
                cp.wait()

            @pl.when(off)
            def _():
                rcopy(ch, ch, send.at[k, 0], recv.at[k], d_lp).wait_recv()

            for i, (cond, d) in enumerate(outs):
                @pl.when(cond)
                def _():
                    rcopy(ch, ch, send.at[k, i], recv.at[k], d).start()

        def finish():
            for k, ch in enumerate(chunks):
                for i, (cond, d) in enumerate(outs):
                    @pl.when(cond)
                    def _():
                        rcopy(ch, ch, send.at[k, i], recv.at[k], d).wait_send()

        return finish

    f0 = tree(0, 0, [t0, nz], [rows.at[0, 0], n_ref], tts, ttr, cl.at[0])
    step = 768 // NCH
    par = lax.div(x, 2)
    f1 = tree(
        lax.rem(x, 2) * 2 + lax.div(zh, 2),
        lax.rem(zh, 2) * 2 + core,
        [cols.at[:, pl.ds(k * step, step), :] for k in range(NCH)],
        [rows.at[:, par, pl.ds(k * step, step), :] for k in range(NCH)],
        tcs_, tcr, cl.at[1],
    )
    f0()
    f1()
    for cp in sends:
        cp.wait_send()


def gather(f, noise):
    DMA = pltpu.SemaphoreType.DMA
    vm = pl.BlockSpec(memory_space=pltpu.VMEM)
    return pl.pallas_call(
        comm_kernel,
        out_shape=(
            jax.ShapeDtypeStruct((4, 2, 768, 128), jnp.bfloat16),
            jax.ShapeDtypeStruct((4, 768, 128), jnp.bfloat16),
            jax.ShapeDtypeStruct((768, 128), jnp.bfloat16),
            jax.ShapeDtypeStruct((8, 128), jnp.float32),
        ),
        in_specs=[vm, vm],
        out_specs=(vm, vm, vm, vm),
        scratch_shapes=[
            DMA((4,)), DMA((4,)), DMA,
            DMA((2, 7)), DMA((2, 7)), DMA((1,)), DMA((1,)),
            DMA((NCH, 4)), DMA((NCH,)),
            DMA((2, 4)), DMA((2,)), DMA((2, NCH)),
        ],
        compiler_params=pltpu.CompilerParams(collective_id=0, has_side_effects=True),
        name="gather_features",
    )(f, noise)


def invert(X, t_ref, w_ref, n_row):
    T = t_ref[...].astype(jnp.float32)
    Tw = T * w_ref[...]
    tsq = jnp.sum(T * Tw, axis=0, keepdims=True)
    hi = Tw.astype(jnp.bfloat16)
    lo = (Tw - hi.astype(jnp.float32)).astype(jnp.bfloat16)
    g = tdot(t_ref[...], hi) + tdot(t_ref[...], lo)
    tcol = jnp.broadcast_to(tsq, (128, 128)).T
    eye = lax.broadcasted_iota(jnp.int32, (128, 128), 0) == lax.broadcasted_iota(jnp.int32, (128, 128), 1)
    k0 = jnp.exp(g - 0.5 * (tcol + tsq)) + jnp.where(eye, n_row, 0.0)
    X[:, :128] = k0
    X[:, 128:] = jnp.where(eye, 1.0, 0.0)


def tdot(a, b):
    return lax.dot_general(a, b, (((0,), (0,)), ((), ())), preferred_element_type=jnp.float32)


def fdot(a, b):
    return lax.dot_general(
        a, b, (((1,), (0,)), ((), ())), precision=lax.Precision.HIGHEST, preferred_element_type=jnp.float32
    )


def eliminate(X, first, count):
    lane = lax.broadcasted_iota(jnp.int32, (128, 128), 1)
    sub = lax.broadcasted_iota(jnp.int32, (128, 1), 0)

    def step(j, _):
        row = X[pl.ds(j, 1), :]
        S = X[:, :128]
        col = jnp.sum(jnp.where(lane == j, S, 0.0), axis=1, keepdims=True)
        d = jnp.sum(jnp.where(lane[:1] == j, row[:, :128], 0.0), axis=1, keepdims=True)
        f = jnp.where(sub > j, col / d, 0.0)
        X[:, :128] = S - f * row[:, :128]
        X[:, 128:] = X[:, 128:] - f * row[:, 128:]
        return 0

    lax.fori_loop(first, first + count, step, 0)


def scaled_inverse(X):
    lane = lax.broadcasted_iota(jnp.int32, (128, 128), 1)
    sub = lax.broadcasted_iota(jnp.int32, (128, 128), 0)
    d = jnp.sum(jnp.where(lane == sub, X[:, :128], 0.0), axis=1, keepdims=True)
    return X[:, 128:] * lax.rsqrt(d)


def slot(t):
    return t


def main_kernel(rows, cols, t0, w_ref, nz, n_ref, pan, out, X, whi, wlo):
    r = lax.axis_index("row")
    c = lax.axis_index("col")
    invert(X, t0, w_ref, nz[0:1, :])
    eliminate(X, 0, 128)
    inv = scaled_inverse(X)
    inv_t = inv.T
    eye = lax.broadcasted_iota(jnp.int32, (128, 128), 0) == lax.broadcasted_iota(jnp.int32, (128, 128), 1)
    w = w_ref[...]

    def split(x, at):
        hi = x.astype(jnp.bfloat16)
        whi[:, at * 128:(at + 1) * 128] = hi
        wlo[:, at * 128:(at + 1) * 128] = (x - hi.astype(jnp.float32)).astype(jnp.bfloat16)

    T = t0[...].astype(jnp.float32)
    Tw = T * w
    split(Tw, 4)
    tsq = jnp.sum(T * Tw, axis=0, keepdims=True)
    tcol = jnp.broadcast_to(tsq, (128, 128)).T
    csq = []
    pct = []
    for u in range(4):
        C = cols[u].astype(jnp.float32)
        Cw = C * w
        split(Cw, u)
        cs = jnp.sum(C * Cw, axis=0, keepdims=True)
        csq.append(cs)
        g = tdot(whi[:, 512:], cols[u]) + tdot(wlo[:, 512:], cols[u])
        kc = jnp.exp(g - 0.5 * (tcol + cs))
        kc = kc + jnp.where(jnp.logical_and(eye, u * 32 + c == 0), nz[0:1, :], 0.0)
        pct.append(fdot(inv, kc))
    sq = jnp.concatenate(csq + [tsq], axis=1)
    pt = jnp.concatenate(pct, axis=1)
    for t in range(8):
        a = rows[slot(t)]
        af = a.astype(jnp.float32)
        asq = jnp.sum(af * af * w, axis=0, keepdims=True)
        acol = jnp.broadcast_to(asq, (128, 128)).T[:, :1]
        g = tdot(a, whi[...]) + tdot(a, wlo[...])
        k = jnp.exp(g - 0.5 * (acol + sq))
        nr = jnp.where(eye, n_ref[t:t + 1, :], 0.0)
        ka = k[:, 512:] + jnp.where(t * 16 + r == 0, nr, 0.0)
        p = fdot(ka, inv_t)
        pan[t] = p
        for u in range(4):
            x = k[:, u * 128:(u + 1) * 128] + jnp.where(t * 16 + r == u * 32 + c, nr, 0.0)
            out[t, :, u, :] = x - fdot(p, pt[:, u * 128:(u + 1) * 128])


def finish(rows, cols, t0, w, nz, noise):
    vm = pl.BlockSpec(memory_space=pltpu.VMEM)
    return pl.pallas_call(
        main_kernel,
        out_shape=(
            jax.ShapeDtypeStruct((8, 128, 128), jnp.float32),
            jax.ShapeDtypeStruct((8, 128, 4, 128), jnp.float32),
        ),
        in_specs=[vm] * 6,
        out_specs=(vm, vm),
        scratch_shapes=[
            pltpu.VMEM((128, 256), jnp.float32),
            pltpu.VMEM((768, 640), jnp.bfloat16),
            pltpu.VMEM((768, 640), jnp.bfloat16),
        ],
        name="panel_step",
    )(rows, cols, t0, w, nz, noise)


def body(features, lengthscale, noise):
    f = jnp.transpose(features, (0, 2, 1)).reshape(4, 2, 24, 128)
    ls = lengthscale.reshape(4, 4, 2, 24).transpose(2, 0, 1, 3).reshape(768)
    w = jnp.broadcast_to((1.0 / (ls * ls))[:, None], (768, 128))
    rows, cols, t0, nz = gather(f, noise)
    return finish(rows.reshape(8, 768, 128), cols, t0, w, nz, noise)


def solution(mesh):
    placed = (P(None, "row", "col"), P(), P(None, "row"))
    return jax.shard_map(
        body,
        mesh=mesh,
        in_specs=placed,
        out_specs=(P(None, "row", None), P(None, "row", None, "col")),
        check_vma=False,
    )
```

```python
import jax
import jax.numpy as jnp
from jax import lax
from jax.experimental import pallas as pl
from jax.experimental.pallas import tpu as pltpu
from jax.sharding import PartitionSpec as P

MESH = pl.DeviceIdType.MESH
NCH = 8


def rcopy(src, dst, ss, rs, dev):
    return pltpu.make_async_remote_copy(
        src_ref=src, dst_ref=dst, send_sem=ss, recv_sem=rs, device_id=dev, device_id_type=MESH
    )


def place():
    r = lax.axis_index("row")
    c = lax.axis_index("col")
    return (
        lax.div(r, 4),
        lax.rem(r, 4),
        lax.div(c, 8),
        lax.rem(lax.div(c, 2), 4),
        lax.rem(c, 2),
    )


def dev(zl, y, x, zh, core):
    return (zl * 4 + y, (x * 4 + zh) * 2 + core)


def comm_kernel(
    f_ref, n_ref, rows, cols, nz,
    s1s, s1r, loc, s2s, s2r, tcs_, tcr, tts, ttr, cl,
):
    zl, y, x, zh, core = place()
    oc = 1 - core
    zp, zm, zo = lax.rem(zh + 1, 4), lax.rem(zh + 3, 4), lax.rem(zh + 2, 4)
    xp, xm, xo = lax.rem(x + 1, 4), lax.rem(x + 3, 4), lax.rem(x + 2, 4)
    yp, ym = lax.rem(y + 1, 4), lax.rem(y + 3, 4)
    lp, lm = lax.rem(zl + 1, 4), lax.rem(zl + 3, 4)
    d_zp, d_zm = dev(zl, y, x, zp, core), dev(zl, y, x, zm, core)
    d_xp, d_xm = dev(zl, y, xp, zh, core), dev(zl, y, xm, zh, core)
    d_co = dev(zl, y, x, zh, oc)
    d_yp, d_ym = dev(zl, yp, x, zh, core), dev(zl, ym, x, zh, core)
    d_lp, d_lm = dev(lp, y, x, zh, core), dev(lm, y, x, zh, core)
    partners = (d_zp, d_zm, d_xp, d_xm, d_co, d_yp, d_ym, d_lp, d_lm)
    bar = pltpu.get_barrier_semaphore()
    for d in partners:
        pl.semaphore_signal(bar, inc=1, device_id=d, device_id_type=MESH)
    pl.semaphore_wait(bar, len(partners))
    turn = 1 - 2 * core
    y_a = lax.rem(y + turn + 4, 4)
    y_b = lax.rem(y - turn + 4, 4)
    d_a, d_b = dev(zl, y_a, x, zh, core), dev(zl, y_b, x, zh, core)
    sends = []

    def go(cp):
        cp.start()
        sends.append(cp)

    def zrow(zz):
        return pl.multiple_of(((core * 4 + x) * 4 + zz) * 24, 8)

    def xrow(kk, xx):
        return pl.multiple_of((kk * 4 + xx) * 96, 32)

    def zblk(zz, par):
        return rows.at[pl.ds(5 * par, 5 - par), pl.ds(zrow(zz), 24), :]

    def blk(kk, xx, par):
        return rows.at[pl.ds(5 * par, 5 - par), pl.ds(xrow(kk, xx), 96), :]

    def tree(zr, yr):
        on = y == yr
        root = jnp.logical_and(on, zl == zr)
        c_up = jnp.logical_and(on, jnp.logical_and(zl >= zr, zl < 3))
        c_dn = jnp.logical_and(on, jnp.logical_and(zl <= zr, zl > 0))
        c_b = jnp.logical_or(on, y == lax.rem(yr - turn + 4, 4))
        return root, ((c_up, d_lp), (c_dn, d_lm), (on, d_a), (c_b, d_b))

    def from_root(tr, src, ch, send, recv, k, lsem):
        root, outs = tr

        @pl.when(root)
        def _():
            for i, (cond, d) in enumerate(outs):
                @pl.when(cond)
                def _():
                    rcopy(src, ch, send.at[k, i], recv.at[k], d).start()
            pltpu.make_async_copy(src, ch, lsem.at[k]).start()

    def onward(tr, ch, send, recv, k):
        root, outs = tr

        @pl.when(jnp.logical_not(root))
        def _():
            rcopy(ch, ch, send.at[k, 0], recv.at[k], d_lp).wait_recv()
            for i, (cond, d) in enumerate(outs):
                @pl.when(cond)
                def _():
                    rcopy(ch, ch, send.at[k, i], recv.at[k], d).start()

    def local(tr, src, ch, k, lsem):
        @pl.when(tr[0])
        def _():
            pltpu.make_async_copy(src, ch, lsem.at[k]).wait()

    def done(tr, ch, send, recv, k):
        for i, (cond, d) in enumerate(tr[1]):
            @pl.when(cond)
            def _():
                rcopy(ch, ch, send.at[k, i], recv.at[k], d).wait_send()

    t0 = tree(0, 0)
    own4 = rows.at[4, pl.ds(zrow(zh), 24), :]
    first = ((f_ref.at[0, 0], own4), (n_ref, nz))
    for k, (src, ch) in enumerate(first):
        from_root(t0, src, ch, tts, ttr, k, cl.at[0])
    even = rows.at[pl.ds(0, 4), pl.ds(zrow(zh), 24), :]
    me0 = pltpu.make_async_copy(f_ref.at[:, 0], even, loc.at[0])
    me1 = pltpu.make_async_copy(f_ref.at[:, 1], zblk(zh, 1), loc.at[1])
    me0.start()
    me1.start()
    go(rcopy(f_ref.at[:, 1], zblk(zh, 1), s1s.at[0], s1r.at[0], d_zp))
    go(rcopy(f_ref.at[:, 1], zblk(zh, 1), s1s.at[1], s1r.at[1], d_zm))
    for k, (src, ch) in enumerate(first):
        onward(t0, ch, tts, ttr, k)
        local(t0, src, ch, k, cl.at[0])
    me0.wait()
    own = zblk(zh, 0)
    go(rcopy(own, own, s1s.at[2], s1r.at[2], d_zp))
    go(rcopy(own, own, s1s.at[3], s1r.at[3], d_zm))

    def z_in(zz, par, i):
        b = zblk(zz, par)
        rcopy(b, b, s1s.at[i], s1r.at[i], d_zp).wait_recv()
        return b

    b = z_in(zp, 1, 1)
    go(rcopy(b, b, s1s.at[5], s1r.at[5], d_zm))
    b = z_in(zm, 0, 2)
    go(rcopy(b, b, s1s.at[4], s1r.at[4], d_zp))
    z_in(zm, 1, 0)
    z_in(zp, 0, 3)
    z_in(zo, 1, 5)
    me1.wait()

    def own_out(par):
        o = blk(core, x, par)
        for i, d in enumerate((d_xp, d_xm, d_co)):
            go(rcopy(o, o, s2s.at[par, i], s2r.at[par, i], d))

    def x_in(xx, par, i, out):
        b = blk(core, xx, par)
        rcopy(b, b, s2s.at[par, i], s2r.at[par, i], d_xp).wait_recv()
        if i == par:
            go(rcopy(b, b, s2s.at[par, 3], s2r.at[par, 3], (d_xp, d_xm)[par]))
        go(rcopy(b, b, s2s.at[par, out], s2r.at[par, out], d_co))

    def co_in(xx, i):
        for par in range(2):
            b = blk(oc, xx, par)
            rcopy(b, b, s2s.at[par, i], s2r.at[par, i], d_co).wait_recv()

    half = lax.div(x, 2)
    tc = tree(lax.rem(x, 2) * 2 + lax.div(zh, 2), lax.rem(zh, 2) * 2 + core)
    order = ((core, x), (oc, x), (core, xm), (core, xp), (oc, xm), (oc, xp), (core, xo), (oc, xo))

    def src_of(k):
        return rows.at[pl.ds(5 * half, 4), pl.ds(xrow(*order[k]), 96), :]

    def dst_of(k):
        return cols.at[:, pl.ds(xrow(*order[k]), 96), :]

    def feed(k):
        from_root(tc, src_of(k), dst_of(k), tcs_, tcr, k, cl.at[1])

    def pass_on(k):
        onward(tc, dst_of(k), tcs_, tcr, k)

    own_out(1)
    z_in(zo, 0, 4)
    own_out(0)
    feed(0)
    for par in (1, 0):
        if par == 0:
            x_in(xm, 0, 0, 4)
            x_in(xp, 0, 1, 5)
        else:
            x_in(xp, 1, 1, 5)
            x_in(xm, 1, 0, 4)
    feed(2)
    feed(3)
    co_in(x, 2)
    feed(1)
    pass_on(0)
    x_in(xo, 1, 3, 6)
    x_in(xo, 0, 3, 6)
    feed(6)
    co_in(xm, 4)
    feed(4)
    co_in(xp, 5)
    feed(5)
    pass_on(2)
    pass_on(3)
    co_in(xo, 6)
    feed(7)
    for k in (1, 6, 4, 5, 7):
        pass_on(k)
    for k in range(NCH):
        local(tc, src_of(k), dst_of(k), k, cl.at[1])
    for k, (src, ch) in enumerate(first):
        done(t0, ch, tts, ttr, k)
    for k in range(NCH):
        done(tc, dst_of(k), tcs_, tcr, k)
    for cp in sends:
        cp.wait_send()


def gather(f, noise):
    DMA = pltpu.SemaphoreType.DMA
    vm = pl.BlockSpec(memory_space=pltpu.VMEM)
    return pl.pallas_call(
        comm_kernel,
        out_shape=(
            jax.ShapeDtypeStruct((9, 768, 128), jnp.bfloat16),
            jax.ShapeDtypeStruct((4, 768, 128), jnp.bfloat16),
            jax.ShapeDtypeStruct((8, 128), jnp.float32),
        ),
        in_specs=[vm, vm],
        out_specs=(vm, vm, vm),
        scratch_shapes=[
            DMA((6,)), DMA((6,)), DMA((2,)),
            DMA((2, 7)), DMA((2, 7)),
            DMA((NCH, 4)), DMA((NCH,)),
            DMA((2, 4)), DMA((2,)), DMA((2, NCH)),
        ],
        compiler_params=pltpu.CompilerParams(collective_id=0, has_side_effects=True),
        name="gather_features",
    )(f, noise)


def invert(X, t_ref, w_ref, n_row):
    T = t_ref[...].astype(jnp.float32)
    Tw = T * w_ref[...]
    tsq = jnp.sum(T * Tw, axis=0, keepdims=True)
    hi = Tw.astype(jnp.bfloat16)
    lo = (Tw - hi.astype(jnp.float32)).astype(jnp.bfloat16)
    g = tdot(t_ref[...], hi) + tdot(t_ref[...], lo)
    tcol = jnp.broadcast_to(tsq, (128, 128)).T
    eye = lax.broadcasted_iota(jnp.int32, (128, 128), 0) == lax.broadcasted_iota(jnp.int32, (128, 128), 1)
    k0 = jnp.exp(g - 0.5 * (tcol + tsq)) + jnp.where(eye, n_row, 0.0)
    X[:, :128] = k0
    X[:, 128:] = jnp.where(eye, 1.0, 0.0)


def tdot(a, b):
    return lax.dot_general(a, b, (((0,), (0,)), ((), ())), preferred_element_type=jnp.float32)


def fdot(a, b):
    return lax.dot_general(
        a, b, (((1,), (0,)), ((), ())), precision=lax.Precision.HIGHEST, preferred_element_type=jnp.float32
    )


def eliminate(X, first, count):
    lane = lax.broadcasted_iota(jnp.int32, (128, 128), 1)
    sub = lax.broadcasted_iota(jnp.int32, (128, 1), 0)

    def step(j, _):
        row = X[pl.ds(j, 1), :]
        S = X[:, :128]
        col = jnp.sum(jnp.where(lane == j, S, 0.0), axis=1, keepdims=True)
        d = jnp.sum(jnp.where(lane[:1] == j, row[:, :128], 0.0), axis=1, keepdims=True)
        f = jnp.where(sub > j, col / d, 0.0)
        X[:, :128] = S - f * row[:, :128]
        X[:, 128:] = X[:, 128:] - f * row[:, 128:]
        return 0

    lax.fori_loop(first, first + count, step, 0)


def scaled_inverse(X):
    lane = lax.broadcasted_iota(jnp.int32, (128, 128), 1)
    sub = lax.broadcasted_iota(jnp.int32, (128, 128), 0)
    d = jnp.sum(jnp.where(lane == sub, X[:, :128], 0.0), axis=1, keepdims=True)
    return X[:, 128:] * lax.rsqrt(d)


def slot(t):
    return 5 * (t % 2) + t // 2


def main_kernel(rows, cols, w_ref, nz, n_ref, pan, out, X, whi, wlo):
    r = lax.axis_index("row")
    c = lax.axis_index("col")
    t0 = rows.at[4]
    invert(X, t0, w_ref, nz[0:1, :])
    eliminate(X, 0, 128)
    inv = scaled_inverse(X)
    inv_t = inv.T
    eye = lax.broadcasted_iota(jnp.int32, (128, 128), 0) == lax.broadcasted_iota(jnp.int32, (128, 128), 1)
    w = w_ref[...]

    def split(x, at):
        hi = x.astype(jnp.bfloat16)
        whi[:, at * 128:(at + 1) * 128] = hi
        wlo[:, at * 128:(at + 1) * 128] = (x - hi.astype(jnp.float32)).astype(jnp.bfloat16)

    T = t0[...].astype(jnp.float32)
    Tw = T * w
    split(Tw, 4)
    tsq = jnp.sum(T * Tw, axis=0, keepdims=True)
    tcol = jnp.broadcast_to(tsq, (128, 128)).T
    csq = []
    pct = []
    for u in range(4):
        C = cols[u].astype(jnp.float32)
        Cw = C * w
        split(Cw, u)
        cs = jnp.sum(C * Cw, axis=0, keepdims=True)
        csq.append(cs)
        g = tdot(whi[:, 512:], cols[u]) + tdot(wlo[:, 512:], cols[u])
        kc = jnp.exp(g - 0.5 * (tcol + cs))
        kc = kc + jnp.where(jnp.logical_and(eye, u * 32 + c == 0), nz[0:1, :], 0.0)
        pct.append(fdot(inv, kc))
    sq = jnp.concatenate(csq + [tsq], axis=1)
    pt = jnp.concatenate(pct, axis=1)
    for t in range(8):
        a = rows[slot(t)]
        af = a.astype(jnp.float32)
        asq = jnp.sum(af * af * w, axis=0, keepdims=True)
        acol = jnp.broadcast_to(asq, (128, 128)).T[:, :1]
        g = tdot(a, whi[...]) + tdot(a, wlo[...])
        k = jnp.exp(g - 0.5 * (acol + sq))
        nr = jnp.where(eye, n_ref[t:t + 1, :], 0.0)
        ka = k[:, 512:] + jnp.where(t * 16 + r == 0, nr, 0.0)
        p = fdot(ka, inv_t)
        pan[t] = p
        for u in range(4):
            x = k[:, u * 128:(u + 1) * 128] + jnp.where(t * 16 + r == u * 32 + c, nr, 0.0)
            out[t, :, u, :] = x - fdot(p, pt[:, u * 128:(u + 1) * 128])


def finish(rows, cols, w, nz, noise):
    vm = pl.BlockSpec(memory_space=pltpu.VMEM)
    return pl.pallas_call(
        main_kernel,
        out_shape=(
            jax.ShapeDtypeStruct((8, 128, 128), jnp.float32),
            jax.ShapeDtypeStruct((8, 128, 4, 128), jnp.float32),
        ),
        in_specs=[vm] * 5,
        out_specs=(vm, vm),
        scratch_shapes=[
            pltpu.VMEM((128, 256), jnp.float32),
            pltpu.VMEM((768, 640), jnp.bfloat16),
            pltpu.VMEM((768, 640), jnp.bfloat16),
        ],
        name="panel_step",
    )(rows, cols, w, nz, noise)


def body(features, lengthscale, noise):
    f = jnp.transpose(features, (0, 2, 1)).reshape(4, 2, 24, 128)
    ls = lengthscale.reshape(4, 4, 2, 24).transpose(2, 0, 1, 3).reshape(768)
    w = jnp.broadcast_to((1.0 / (ls * ls))[:, None], (768, 128))
    rows, cols, nz = gather(f, noise)
    return finish(rows, cols, w, nz, noise)


def solution(mesh):
    placed = (P(None, "row", "col"), P(), P(None, "row"))
    return jax.shard_map(
        body,
        mesh=mesh,
        in_specs=placed,
        out_specs=(P(None, "row", None), P(None, "row", None, "col")),
        check_vma=False,
    )
```

```python
import jax
import jax.numpy as jnp
from jax import lax
from jax.experimental import pallas as pl
from jax.experimental.pallas import tpu as pltpu
from jax.sharding import PartitionSpec as P

MESH = pl.DeviceIdType.MESH
NCH = 8


def rcopy(src, dst, ss, rs, dev):
    return pltpu.make_async_remote_copy(
        src_ref=src, dst_ref=dst, send_sem=ss, recv_sem=rs, device_id=dev, device_id_type=MESH
    )


def place():
    r = lax.axis_index("row")
    c = lax.axis_index("col")
    return (
        lax.div(r, 4),
        lax.rem(r, 4),
        lax.div(c, 8),
        lax.rem(lax.div(c, 2), 4),
        lax.rem(c, 2),
    )


def dev(zl, y, x, zh, core):
    return (zl * 4 + y, (x * 4 + zh) * 2 + core)


def comm_kernel(
    f_ref, n_ref, w_ref, rows, cols, nz, X,
    s1s, s1r, loc, s2s, s2r, tcs_, tcr, tts, ttr, cl,
):
    zl, y, x, zh, core = place()
    oc = 1 - core
    zp, zm, zo = lax.rem(zh + 1, 4), lax.rem(zh + 3, 4), lax.rem(zh + 2, 4)
    xp, xm, xo = lax.rem(x + 1, 4), lax.rem(x + 3, 4), lax.rem(x + 2, 4)
    yp, ym = lax.rem(y + 1, 4), lax.rem(y + 3, 4)
    lp, lm = lax.rem(zl + 1, 4), lax.rem(zl + 3, 4)
    d_zp, d_zm = dev(zl, y, x, zp, core), dev(zl, y, x, zm, core)
    d_xp, d_xm = dev(zl, y, xp, zh, core), dev(zl, y, xm, zh, core)
    d_co = dev(zl, y, x, zh, oc)
    d_yp, d_ym = dev(zl, yp, x, zh, core), dev(zl, ym, x, zh, core)
    d_lp, d_lm = dev(lp, y, x, zh, core), dev(lm, y, x, zh, core)
    partners = (d_zp, d_zm, d_xp, d_xm, d_co, d_yp, d_ym, d_lp, d_lm)
    bar = pltpu.get_barrier_semaphore()
    for d in partners:
        pl.semaphore_signal(bar, inc=1, device_id=d, device_id_type=MESH)
    pl.semaphore_wait(bar, len(partners))
    turn = 1 - 2 * core
    y_a = lax.rem(y + turn + 4, 4)
    y_b = lax.rem(y - turn + 4, 4)
    d_a, d_b = dev(zl, y_a, x, zh, core), dev(zl, y_b, x, zh, core)
    sends = []

    def go(cp):
        cp.start()
        sends.append(cp)

    def zrow(zz):
        return pl.multiple_of(((core * 4 + x) * 4 + zz) * 24, 8)

    def xrow(kk, xx):
        return pl.multiple_of((kk * 4 + xx) * 96, 32)

    def zblk(zz, par):
        return rows.at[pl.ds(5 * par, 5 - par), pl.ds(zrow(zz), 24), :]

    def blk(kk, xx, par):
        return rows.at[pl.ds(5 * par, 5 - par), pl.ds(xrow(kk, xx), 96), :]

    def tree(zr, yr):
        on = y == yr
        root = jnp.logical_and(on, zl == zr)
        c_up = jnp.logical_and(on, jnp.logical_and(zl >= zr, zl < 3))
        c_dn = jnp.logical_and(on, jnp.logical_and(zl <= zr, zl > 0))
        c_b = jnp.logical_or(on, y == lax.rem(yr - turn + 4, 4))
        return root, ((c_up, d_lp), (c_dn, d_lm), (on, d_a), (c_b, d_b))

    def from_root(tr, src, ch, send, recv, k, lsem):
        root, outs = tr

        @pl.when(root)
        def _():
            for i, (cond, d) in enumerate(outs):
                @pl.when(cond)
                def _():
                    rcopy(src, ch, send.at[k, i], recv.at[k], d).start()
            pltpu.make_async_copy(src, ch, lsem.at[k]).start()

    def onward(tr, ch, send, recv, k):
        root, outs = tr

        @pl.when(jnp.logical_not(root))
        def _():
            rcopy(ch, ch, send.at[k, 0], recv.at[k], d_lp).wait_recv()
            for i, (cond, d) in enumerate(outs):
                @pl.when(cond)
                def _():
                    rcopy(ch, ch, send.at[k, i], recv.at[k], d).start()

    def local(tr, src, ch, k, lsem):
        @pl.when(tr[0])
        def _():
            pltpu.make_async_copy(src, ch, lsem.at[k]).wait()

    def done(tr, ch, send, recv, k):
        for i, (cond, d) in enumerate(tr[1]):
            @pl.when(cond)
            def _():
                rcopy(ch, ch, send.at[k, i], recv.at[k], d).wait_send()

    t0 = tree(0, 0)
    own4 = rows.at[4, pl.ds(zrow(zh), 24), :]
    first = ((f_ref.at[0, 0], own4), (n_ref, nz))
    for k, (src, ch) in enumerate(first):
        from_root(t0, src, ch, tts, ttr, k, cl.at[0])
    even = rows.at[pl.ds(0, 4), pl.ds(zrow(zh), 24), :]
    me0 = pltpu.make_async_copy(f_ref.at[:, 0], even, loc.at[0])
    me1 = pltpu.make_async_copy(f_ref.at[:, 1], zblk(zh, 1), loc.at[1])
    me0.start()
    me1.start()
    go(rcopy(f_ref.at[:, 1], zblk(zh, 1), s1s.at[0], s1r.at[0], d_zp))
    go(rcopy(f_ref.at[:, 1], zblk(zh, 1), s1s.at[1], s1r.at[1], d_zm))
    for k, (src, ch) in enumerate(first):
        onward(t0, ch, tts, ttr, k)
        local(t0, src, ch, k, cl.at[0])
    me0.wait()
    own = zblk(zh, 0)
    go(rcopy(own, own, s1s.at[2], s1r.at[2], d_zp))
    go(rcopy(own, own, s1s.at[3], s1r.at[3], d_zm))

    def z_in(zz, par, i):
        b = zblk(zz, par)
        rcopy(b, b, s1s.at[i], s1r.at[i], d_zp).wait_recv()
        return b

    b = z_in(zp, 1, 1)
    go(rcopy(b, b, s1s.at[5], s1r.at[5], d_zm))
    b = z_in(zm, 0, 2)
    go(rcopy(b, b, s1s.at[4], s1r.at[4], d_zp))
    z_in(zm, 1, 0)
    z_in(zp, 0, 3)
    z_in(zo, 1, 5)
    me1.wait()

    def own_out(par):
        o = blk(core, x, par)
        for i, d in enumerate((d_xp, d_xm, d_co)):
            go(rcopy(o, o, s2s.at[par, i], s2r.at[par, i], d))

    def x_in(xx, par, i, out):
        b = blk(core, xx, par)
        rcopy(b, b, s2s.at[par, i], s2r.at[par, i], d_xp).wait_recv()
        if i == par:
            go(rcopy(b, b, s2s.at[par, 3], s2r.at[par, 3], (d_xp, d_xm)[par]))
        go(rcopy(b, b, s2s.at[par, out], s2r.at[par, out], d_co))

    def co_in(xx, i):
        for par in range(2):
            b = blk(oc, xx, par)
            rcopy(b, b, s2s.at[par, i], s2r.at[par, i], d_co).wait_recv()

    half = lax.div(x, 2)
    tc = tree(lax.rem(x, 2) * 2 + lax.div(zh, 2), lax.rem(zh, 2) * 2 + core)
    order = ((core, x), (oc, x), (core, xm), (core, xp), (oc, xm), (oc, xp), (core, xo), (oc, xo))

    def src_of(k):
        return rows.at[pl.ds(5 * half, 4), pl.ds(xrow(*order[k]), 96), :]

    def dst_of(k):
        return cols.at[:, pl.ds(xrow(*order[k]), 96), :]

    def feed(k):
        from_root(tc, src_of(k), dst_of(k), tcs_, tcr, k, cl.at[1])

    def pass_on(k):
        onward(tc, dst_of(k), tcs_, tcr, k)

    own_out(1)
    z_in(zo, 0, 4)
    own_out(0)
    feed(0)
    for par in (1, 0):
        if par == 0:
            x_in(xm, 0, 0, 4)
            x_in(xp, 0, 1, 5)
        else:
            x_in(xp, 1, 1, 5)
            x_in(xm, 1, 0, 4)
    feed(2)
    feed(3)
    co_in(x, 2)
    feed(1)
    pass_on(0)
    x_in(xo, 1, 3, 6)
    x_in(xo, 0, 3, 6)
    feed(6)
    co_in(xm, 4)
    feed(4)
    co_in(xp, 5)
    feed(5)
    pass_on(2)
    pass_on(3)
    co_in(xo, 6)
    feed(7)
    invert(X, rows.at[4], w_ref, nz[0:1, :])
    eliminate(X, 0, 16)
    for n, k in enumerate((1, 6, 4, 5)):
        pass_on(k)
        eliminate(X, 16 + 12 * n, 12)
    pass_on(7)
    for k in range(NCH):
        local(tc, src_of(k), dst_of(k), k, cl.at[1])
    for k, (src, ch) in enumerate(first):
        done(t0, ch, tts, ttr, k)
    for k in range(NCH):
        done(tc, dst_of(k), tcs_, tcr, k)
    for cp in sends:
        cp.wait_send()


def gather(f, noise, w):
    DMA = pltpu.SemaphoreType.DMA
    vm = pl.BlockSpec(memory_space=pltpu.VMEM)
    return pl.pallas_call(
        comm_kernel,
        out_shape=(
            jax.ShapeDtypeStruct((9, 768, 128), jnp.bfloat16),
            jax.ShapeDtypeStruct((4, 768, 128), jnp.bfloat16),
            jax.ShapeDtypeStruct((8, 128), jnp.float32),
            jax.ShapeDtypeStruct((128, 256), jnp.float32),
        ),
        in_specs=[vm, vm, vm],
        out_specs=(vm, vm, vm, vm),
        scratch_shapes=[
            DMA((6,)), DMA((6,)), DMA((2,)),
            DMA((2, 7)), DMA((2, 7)),
            DMA((NCH, 4)), DMA((NCH,)),
            DMA((2, 4)), DMA((2,)), DMA((2, NCH)),
        ],
        compiler_params=pltpu.CompilerParams(collective_id=0, has_side_effects=True),
        name="gather_features",
    )(f, noise, w)


def invert(X, t_ref, w_ref, n_row):
    T = t_ref[...].astype(jnp.float32)
    Tw = T * w_ref[...]
    tsq = jnp.sum(T * Tw, axis=0, keepdims=True)
    hi = Tw.astype(jnp.bfloat16)
    lo = (Tw - hi.astype(jnp.float32)).astype(jnp.bfloat16)
    g = tdot(t_ref[...], hi) + tdot(t_ref[...], lo)
    tcol = jnp.broadcast_to(tsq, (128, 128)).T
    eye = lax.broadcasted_iota(jnp.int32, (128, 128), 0) == lax.broadcasted_iota(jnp.int32, (128, 128), 1)
    k0 = jnp.exp(g - 0.5 * (tcol + tsq)) + jnp.where(eye, n_row, 0.0)
    X[:, :128] = k0
    X[:, 128:] = jnp.where(eye, 1.0, 0.0)


def tdot(a, b):
    return lax.dot_general(a, b, (((0,), (0,)), ((), ())), preferred_element_type=jnp.float32)


def fdot(a, b):
    return lax.dot_general(
        a, b, (((1,), (0,)), ((), ())), precision=lax.Precision.HIGHEST, preferred_element_type=jnp.float32
    )


def eliminate(X, first, count):
    lane = lax.broadcasted_iota(jnp.int32, (128, 128), 1)
    sub = lax.broadcasted_iota(jnp.int32, (128, 1), 0)

    def at(row, j):
        return jnp.sum(jnp.where(lane[:1] == j, row[:, :128], 0.0), axis=1, keepdims=True)

    def step(i, _):
        j = 2 * i
        S = X[:, :128]
        r0 = X[pl.ds(j, 1), :]
        r1 = X[pl.ds(j + 1, 1), :]
        c0 = jnp.sum(jnp.where(lane == j, S, 0.0), axis=1, keepdims=True)
        c1 = jnp.sum(jnp.where(lane == j + 1, S, 0.0), axis=1, keepdims=True)
        s01 = at(r0, j + 1)
        i0 = 1.0 / at(r0, j)
        a = s01 * i0
        i1 = 1.0 / (at(r1, j + 1) - s01 * a)
        r1 = r1 - a * r0
        f0 = jnp.where(sub > j, c0 * i0, 0.0)
        f1 = jnp.where(sub > j + 1, (c1 - c0 * a) * i1, 0.0)
        X[:, :128] = S - f0 * r0[:, :128] - f1 * r1[:, :128]
        X[:, 128:] = X[:, 128:] - f0 * r0[:, 128:] - f1 * r1[:, 128:]
        return 0

    lax.fori_loop(first, first + count, step, 0)


def scaled_inverse(X):
    lane = lax.broadcasted_iota(jnp.int32, (128, 128), 1)
    sub = lax.broadcasted_iota(jnp.int32, (128, 128), 0)
    d = jnp.sum(jnp.where(lane == sub, X[:, :128], 0.0), axis=1, keepdims=True)
    return X[:, 128:] * lax.rsqrt(d)


def slot(t):
    return 5 * (t % 2) + t // 2


def main_kernel(rows, cols, w_ref, nz, n_ref, X, pan, out, whi, wlo):
    r = lax.axis_index("row")
    c = lax.axis_index("col")
    t0 = rows.at[4]
    inv = scaled_inverse(X)
    inv_t = inv.T
    eye = lax.broadcasted_iota(jnp.int32, (128, 128), 0) == lax.broadcasted_iota(jnp.int32, (128, 128), 1)
    w = w_ref[...]

    def split(x, at):
        hi = x.astype(jnp.bfloat16)
        whi[:, at * 128:(at + 1) * 128] = hi
        wlo[:, at * 128:(at + 1) * 128] = (x - hi.astype(jnp.float32)).astype(jnp.bfloat16)

    T = t0[...].astype(jnp.float32)
    Tw = T * w
    split(Tw, 4)
    tsq = jnp.sum(T * Tw, axis=0, keepdims=True)
    tcol = jnp.broadcast_to(tsq, (128, 128)).T
    csq = []
    pct = []
    for u in range(4):
        C = cols[u].astype(jnp.float32)
        Cw = C * w
        split(Cw, u)
        cs = jnp.sum(C * Cw, axis=0, keepdims=True)
        csq.append(cs)
        g = tdot(whi[:, 512:], cols[u]) + tdot(wlo[:, 512:], cols[u])
        kc = jnp.exp(g - 0.5 * (tcol + cs))
        kc = kc + jnp.where(jnp.logical_and(eye, u * 32 + c == 0), nz[0:1, :], 0.0)
        pct.append(fdot(inv, kc))
    sq = jnp.concatenate(csq + [tsq], axis=1)
    pt = jnp.concatenate(pct, axis=1)
    for t in range(8):
        a = rows[slot(t)]
        af = a.astype(jnp.float32)
        asq = jnp.sum(af * af * w, axis=0, keepdims=True)
        acol = jnp.broadcast_to(asq, (128, 128)).T[:, :1]
        g = tdot(a, whi[...]) + tdot(a, wlo[...])
        k = jnp.exp(g - 0.5 * (acol + sq))
        nr = jnp.where(eye, n_ref[t:t + 1, :], 0.0)
        ka = k[:, 512:] + jnp.where(t * 16 + r == 0, nr, 0.0)
        p = fdot(ka, inv_t)
        pan[t] = p
        for u in range(4):
            x = k[:, u * 128:(u + 1) * 128] + jnp.where(t * 16 + r == u * 32 + c, nr, 0.0)
            out[t, :, u, :] = x - fdot(p, pt[:, u * 128:(u + 1) * 128])


def finish(rows, cols, w, nz, noise, X):
    vm = pl.BlockSpec(memory_space=pltpu.VMEM)
    return pl.pallas_call(
        main_kernel,
        out_shape=(
            jax.ShapeDtypeStruct((8, 128, 128), jnp.float32),
            jax.ShapeDtypeStruct((8, 128, 4, 128), jnp.float32),
        ),
        in_specs=[vm] * 6,
        out_specs=(vm, vm),
        scratch_shapes=[
            pltpu.VMEM((768, 640), jnp.bfloat16),
            pltpu.VMEM((768, 640), jnp.bfloat16),
        ],
        name="panel_step",
    )(rows, cols, w, nz, noise, X)


def body(features, lengthscale, noise):
    f = jnp.transpose(features, (0, 2, 1)).reshape(4, 2, 24, 128)
    ls = lengthscale.reshape(4, 4, 2, 24).transpose(2, 0, 1, 3).reshape(768)
    w = jnp.broadcast_to((1.0 / (ls * ls))[:, None], (768, 128))
    rows, cols, nz, X = gather(f, noise, w)
    return finish(rows, cols, w, nz, noise, X)


def solution(mesh):
    placed = (P(None, "row", "col"), P(), P(None, "row"))
    return jax.shard_map(
        body,
        mesh=mesh,
        in_specs=placed,
        out_specs=(P(None, "row", None), P(None, "row", None, "col")),
        check_vma=False,
    )
```

```python
import jax
import jax.numpy as jnp
from jax import lax
from jax.experimental import pallas as pl
from jax.experimental.pallas import tpu as pltpu
from jax.sharding import PartitionSpec as P

MESH = pl.DeviceIdType.MESH
NCH = 8


def rcopy(src, dst, ss, rs, dev):
    return pltpu.make_async_remote_copy(
        src_ref=src, dst_ref=dst, send_sem=ss, recv_sem=rs, device_id=dev, device_id_type=MESH
    )


def place():
    r = lax.axis_index("row")
    c = lax.axis_index("col")
    return (
        lax.div(r, 4),
        lax.rem(r, 4),
        lax.div(c, 8),
        lax.rem(lax.div(c, 2), 4),
        lax.rem(c, 2),
    )


def dev(zl, y, x, zh, core):
    return (zl * 4 + y, (x * 4 + zh) * 2 + core)


def comm_kernel(
    f_ref, n_ref, w_ref, rows, cols, nz, X,
    s1s, s1r, loc, s2s, s2r, tcs_, tcr, tts, ttr, cl, ps, pr,
):
    zl, y, x, zh, core = place()
    oc = 1 - core
    zp, zm, zo = lax.rem(zh + 1, 4), lax.rem(zh + 3, 4), lax.rem(zh + 2, 4)
    xp, xm, xo = lax.rem(x + 1, 4), lax.rem(x + 3, 4), lax.rem(x + 2, 4)
    yp, ym = lax.rem(y + 1, 4), lax.rem(y + 3, 4)
    lp, lm = lax.rem(zl + 1, 4), lax.rem(zl + 3, 4)
    d_zp, d_zm = dev(zl, y, x, zp, core), dev(zl, y, x, zm, core)
    d_xp, d_xm = dev(zl, y, xp, zh, core), dev(zl, y, xm, zh, core)
    d_co = dev(zl, y, x, zh, oc)
    d_yp, d_ym = dev(zl, yp, x, zh, core), dev(zl, ym, x, zh, core)
    d_lp, d_lm = dev(lp, y, x, zh, core), dev(lm, y, x, zh, core)
    partners = (d_zp, d_zm, d_xp, d_xm, d_co, d_yp, d_ym, d_lp, d_lm)
    bar = pltpu.get_barrier_semaphore()
    for d in partners:
        pl.semaphore_signal(bar, inc=1, device_id=d, device_id_type=MESH)
    pl.semaphore_wait(bar, len(partners))
    turn = 1 - 2 * core
    y_a = lax.rem(y + turn + 4, 4)
    y_b = lax.rem(y - turn + 4, 4)
    d_a, d_b = dev(zl, y_a, x, zh, core), dev(zl, y_b, x, zh, core)
    sends = []

    def go(cp):
        cp.start()
        sends.append(cp)

    def zrow(zz):
        return pl.multiple_of(((core * 4 + x) * 4 + zz) * 24, 8)

    def xrow(kk, xx):
        return pl.multiple_of((kk * 4 + xx) * 96, 32)

    def zblk(zz, par):
        return rows.at[pl.ds(5 * par, 4), pl.ds(zrow(zz), 24), :]

    def blk(kk, xx, par):
        return rows.at[pl.ds(5 * par, 4), pl.ds(xrow(kk, xx), 96), :]

    def tree(zr, yr):
        on = y == yr
        root = jnp.logical_and(on, zl == zr)
        c_up = jnp.logical_and(on, jnp.logical_and(zl >= zr, zl < 3))
        c_dn = jnp.logical_and(on, jnp.logical_and(zl <= zr, zl > 0))
        c_b = jnp.logical_or(on, y == lax.rem(yr - turn + 4, 4))
        return root, ((c_up, d_lp), (c_dn, d_lm), (on, d_a), (c_b, d_b))

    def from_root(tr, src, ch, send, recv, k, lsem):
        root, outs = tr

        @pl.when(root)
        def _():
            for i, (cond, d) in enumerate(outs):
                @pl.when(cond)
                def _():
                    rcopy(src, ch, send.at[k, i], recv.at[k], d).start()
            pltpu.make_async_copy(src, ch, lsem.at[k]).start()

    def onward(tr, ch, send, recv, k):
        root, outs = tr

        @pl.when(jnp.logical_not(root))
        def _():
            rcopy(ch, ch, send.at[k, 0], recv.at[k], d_lp).wait_recv()
            for i, (cond, d) in enumerate(outs):
                @pl.when(cond)
                def _():
                    rcopy(ch, ch, send.at[k, i], recv.at[k], d).start()

    def local(tr, src, ch, k, lsem):
        @pl.when(tr[0])
        def _():
            pltpu.make_async_copy(src, ch, lsem.at[k]).wait()

    def done(tr, ch, send, recv, k):
        for i, (cond, d) in enumerate(tr[1]):
            @pl.when(cond)
            def _():
                rcopy(ch, ch, send.at[k, i], recv.at[k], d).wait_send()

    t0 = tree(0, 0)
    own4 = rows.at[4, pl.ds(zrow(zh), 24), :]
    first = ((f_ref.at[0, 0], own4), (n_ref, nz))
    for k, (src, ch) in enumerate(first):
        from_root(t0, src, ch, tts, ttr, k, cl.at[0])
    keep = []
    for par in (1, 0):
        me = pltpu.make_async_copy(f_ref.at[:, par], zblk(zh, par), loc.at[par])
        me.start()
        keep.append(me)
        for i, d in enumerate((d_zp, d_zm)):
            n = 2 * (1 - par) + i
            go(rcopy(f_ref.at[:, par], zblk(zh, par), s1s.at[n], s1r.at[n], d))

    def z_in(zz, par, i):
        b = zblk(zz, par)
        rcopy(b, b, s1s.at[i], s1r.at[i], d_zp).wait_recv()
        return b

    b = z_in(zp, 1, 1)
    go(rcopy(b, b, s1s.at[5], s1r.at[5], d_zm))
    b = z_in(zm, 0, 2)
    go(rcopy(b, b, s1s.at[4], s1r.at[4], d_zp))
    for k, (src, ch) in enumerate(first):
        onward(t0, ch, tts, ttr, k)
        local(t0, src, ch, k, cl.at[0])

    def tz(zz):
        return rows.at[4, pl.ds(zrow(zz), 24), :]

    def tx(kk, xx):
        return rows.at[4, pl.ds(xrow(kk, xx), 96), :]

    def t_out(b, i, d):
        go(rcopy(b, b, ps.at[i], pr.at[i], d))

    def t_in(b, i):
        rcopy(b, b, ps.at[i], pr.at[i], d_co).wait_recv()
        return b

    t_out(own4, 0, d_zp)
    t_out(own4, 1, d_zm)
    z_in(zm, 1, 0)
    z_in(zp, 0, 3)
    z_in(zo, 1, 5)
    for me in keep:
        me.wait()

    def own_out(par):
        o = blk(core, x, par)
        for i, d in enumerate((d_xp, d_xm, d_co)):
            go(rcopy(o, o, s2s.at[par, i], s2r.at[par, i], d))

    def x_in(xx, par, i, out):
        b = blk(core, xx, par)
        rcopy(b, b, s2s.at[par, i], s2r.at[par, i], d_xp).wait_recv()
        if i == par:
            go(rcopy(b, b, s2s.at[par, 3], s2r.at[par, 3], (d_xp, d_xm)[par]))
        go(rcopy(b, b, s2s.at[par, out], s2r.at[par, out], d_co))

    def co_in(xx, i):
        for par in range(2):
            b = blk(oc, xx, par)
            rcopy(b, b, s2s.at[par, i], s2r.at[par, i], d_co).wait_recv()

    half = lax.div(x, 2)
    tc = tree(lax.rem(x, 2) * 2 + lax.div(zh, 2), lax.rem(zh, 2) * 2 + core)
    order = ((core, x), (oc, x), (core, xm), (core, xp), (oc, xm), (oc, xp), (core, xo), (oc, xo))

    def src_of(k):
        return rows.at[pl.ds(5 * half, 4), pl.ds(xrow(*order[k]), 96), :]

    def dst_of(k):
        return cols.at[:, pl.ds(xrow(*order[k]), 96), :]

    def feed(k):
        from_root(tc, src_of(k), dst_of(k), tcs_, tcr, k, cl.at[1])

    def pass_on(k):
        onward(tc, dst_of(k), tcs_, tcr, k)

    own_out(1)
    z_in(zo, 0, 4)
    own_out(0)
    feed(0)
    t_out(t_in(tz(zm), 0), 2, d_zp)
    t_in(tz(zp), 1)
    for par in (1, 0):
        if par == 0:
            x_in(xm, 0, 0, 4)
            x_in(xp, 0, 1, 5)
        else:
            x_in(xp, 1, 1, 5)
            x_in(xm, 1, 0, 4)
    feed(2)
    feed(3)
    t_in(tz(zo), 2)
    for i, d in ((3, d_xp), (4, d_xm), (5, d_co)):
        t_out(tx(core, x), i, d)
    co_in(x, 2)
    feed(1)
    pass_on(0)
    x_in(xo, 1, 3, 6)
    x_in(xo, 0, 3, 6)
    feed(6)
    t_in(tx(core, xm), 3)
    t_out(tx(core, xm), 6, d_xp)
    t_out(tx(core, xm), 7, d_co)
    t_out(t_in(tx(core, xp), 4), 8, d_co)
    co_in(xm, 4)
    feed(4)
    co_in(xp, 5)
    feed(5)
    pass_on(2)
    pass_on(3)
    t_out(t_in(tx(core, xo), 6), 9, d_co)
    co_in(xo, 6)
    feed(7)
    for xx, i in ((x, 5), (xm, 7), (xp, 8), (xo, 9)):
        t_in(tx(oc, xx), i)
    invert(X, rows.at[4], w_ref, nz[0:1, :])
    eliminate(X, 0, 16)
    for n, k in enumerate((1, 6, 4, 5)):
        pass_on(k)
        eliminate(X, 16 + 12 * n, 12)
    pass_on(7)
    for k in range(NCH):
        local(tc, src_of(k), dst_of(k), k, cl.at[1])
    for k, (src, ch) in enumerate(first):
        done(t0, ch, tts, ttr, k)
    for k in range(NCH):
        done(tc, dst_of(k), tcs_, tcr, k)
    for cp in sends:
        cp.wait_send()


def gather(f, noise, w):
    DMA = pltpu.SemaphoreType.DMA
    vm = pl.BlockSpec(memory_space=pltpu.VMEM)
    return pl.pallas_call(
        comm_kernel,
        out_shape=(
            jax.ShapeDtypeStruct((9, 768, 128), jnp.bfloat16),
            jax.ShapeDtypeStruct((4, 768, 128), jnp.bfloat16),
            jax.ShapeDtypeStruct((8, 128), jnp.float32),
            jax.ShapeDtypeStruct((128, 256), jnp.float32),
        ),
        in_specs=[vm, vm, vm],
        out_specs=(vm, vm, vm, vm),
        scratch_shapes=[
            DMA((6,)), DMA((6,)), DMA((2,)),
            DMA((2, 7)), DMA((2, 7)),
            DMA((NCH, 4)), DMA((NCH,)),
            DMA((2, 4)), DMA((2,)), DMA((2, NCH)),
            DMA((10,)), DMA((10,)),
        ],
        compiler_params=pltpu.CompilerParams(collective_id=0, has_side_effects=True),
        name="gather_features",
    )(f, noise, w)


def invert(X, t_ref, w_ref, n_row):
    T = t_ref[...].astype(jnp.float32)
    Tw = T * w_ref[...]
    tsq = jnp.sum(T * Tw, axis=0, keepdims=True)
    hi = Tw.astype(jnp.bfloat16)
    lo = (Tw - hi.astype(jnp.float32)).astype(jnp.bfloat16)
    g = tdot(t_ref[...], hi) + tdot(t_ref[...], lo)
    tcol = jnp.broadcast_to(tsq, (128, 128)).T
    eye = lax.broadcasted_iota(jnp.int32, (128, 128), 0) == lax.broadcasted_iota(jnp.int32, (128, 128), 1)
    k0 = jnp.exp(g - 0.5 * (tcol + tsq)) + jnp.where(eye, n_row, 0.0)
    X[:, :128] = k0
    X[:, 128:] = jnp.where(eye, 1.0, 0.0)


def tdot(a, b):
    return lax.dot_general(a, b, (((0,), (0,)), ((), ())), preferred_element_type=jnp.float32)


def fdot(a, b):
    return lax.dot_general(
        a, b, (((1,), (0,)), ((), ())), precision=lax.Precision.HIGHEST, preferred_element_type=jnp.float32
    )


def eliminate(X, first, count):
    lane = lax.broadcasted_iota(jnp.int32, (128, 128), 1)
    sub = lax.broadcasted_iota(jnp.int32, (128, 1), 0)

    def at(row, j):
        return jnp.sum(jnp.where(lane[:1] == j, row[:, :128], 0.0), axis=1, keepdims=True)

    def step(i, _):
        j = 2 * i
        S = X[:, :128]
        r0 = X[pl.ds(j, 1), :]
        r1 = X[pl.ds(j + 1, 1), :]
        c0 = jnp.sum(jnp.where(lane == j, S, 0.0), axis=1, keepdims=True)
        c1 = jnp.sum(jnp.where(lane == j + 1, S, 0.0), axis=1, keepdims=True)
        s01 = at(r0, j + 1)
        i0 = 1.0 / at(r0, j)
        a = s01 * i0
        i1 = 1.0 / (at(r1, j + 1) - s01 * a)
        r1 = r1 - a * r0
        f0 = jnp.where(sub > j, c0 * i0, 0.0)
        f1 = jnp.where(sub > j + 1, (c1 - c0 * a) * i1, 0.0)
        X[:, :128] = S - f0 * r0[:, :128] - f1 * r1[:, :128]
        X[:, 128:] = X[:, 128:] - f0 * r0[:, 128:] - f1 * r1[:, 128:]
        return 0

    lax.fori_loop(first, first + count, step, 0)


def scaled_inverse(X):
    lane = lax.broadcasted_iota(jnp.int32, (128, 128), 1)
    sub = lax.broadcasted_iota(jnp.int32, (128, 128), 0)
    d = jnp.sum(jnp.where(lane == sub, X[:, :128], 0.0), axis=1, keepdims=True)
    return X[:, 128:] * lax.rsqrt(d)


def main_kernel(rows, t0_ref, cols, w_ref, nz, n_ref, X, pan, out, whi, wlo, inv_t, pt, sq):
    r = lax.axis_index("row")
    c = lax.axis_index("col")
    t = pl.program_id(0)
    eye = lax.broadcasted_iota(jnp.int32, (128, 128), 0) == lax.broadcasted_iota(jnp.int32, (128, 128), 1)

    @pl.when(t == 0)
    def _():
        w = w_ref[...]

        def split(x, at):
            hi = x.astype(jnp.bfloat16)
            whi[:, at * 128:(at + 1) * 128] = hi
            wlo[:, at * 128:(at + 1) * 128] = (x - hi.astype(jnp.float32)).astype(jnp.bfloat16)

        inv = scaled_inverse(X)
        inv_t[...] = inv.T
        T = t0_ref[0].astype(jnp.float32)
        Tw = T * w
        split(Tw, 4)
        tsq = jnp.sum(T * Tw, axis=0, keepdims=True)
        sq[:, 512:] = tsq
        tcol = jnp.broadcast_to(tsq, (128, 128)).T
        for u in range(4):
            C = cols[u].astype(jnp.float32)
            Cw = C * w
            split(Cw, u)
            cs = jnp.sum(C * Cw, axis=0, keepdims=True)
            sq[:, u * 128:(u + 1) * 128] = cs
            g = tdot(whi[:, 512:], cols[u]) + tdot(wlo[:, 512:], cols[u])
            kc = jnp.exp(g - 0.5 * (tcol + cs))
            kc = kc + jnp.where(jnp.logical_and(eye, u * 32 + c == 0), nz[0:1, :], 0.0)
            pt[:, u * 128:(u + 1) * 128] = fdot(inv, kc)

    a = rows[0]
    af = a.astype(jnp.float32)
    asq = jnp.sum(af * af * w_ref[...], axis=0, keepdims=True)
    acol = jnp.broadcast_to(asq, (128, 128)).T[:, :1]
    g = tdot(a, whi[...]) + tdot(a, wlo[...])
    k = jnp.exp(g - 0.5 * (acol + sq[...]))
    nr = jnp.where(eye, n_ref[pl.ds(t, 1), :], 0.0)
    ka = k[:, 512:] + jnp.where(t * 16 + r == 0, nr, 0.0)
    p = fdot(ka, inv_t[...])
    pan[0] = p
    for u in range(4):
        x = k[:, u * 128:(u + 1) * 128] + jnp.where(t * 16 + r == u * 32 + c, nr, 0.0)
        out[0, :, u, :] = x - fdot(p, pt[:, u * 128:(u + 1) * 128])


def finish(rows, cols, w, nz, noise, X):
    def whole(*shape):
        return pl.BlockSpec(shape, lambda t: (0,) * len(shape), pipeline_mode=pl.Buffered(1))

    return pl.pallas_call(
        main_kernel,
        grid=(8,),
        out_shape=(
            jax.ShapeDtypeStruct((8, 128, 128), jnp.float32),
            jax.ShapeDtypeStruct((8, 128, 4, 128), jnp.float32),
        ),
        in_specs=[
            pl.BlockSpec((1, 768, 128), lambda t: (5 * (t % 2) + t // 2, 0, 0)),
            pl.BlockSpec((1, 768, 128), lambda t: (4, 0, 0), pipeline_mode=pl.Buffered(1)),
            whole(4, 768, 128), whole(768, 128), whole(8, 128), whole(8, 128), whole(128, 256),
        ],
        out_specs=(
            pl.BlockSpec((1, 128, 128), lambda t: (t, 0, 0)),
            pl.BlockSpec((1, 128, 4, 128), lambda t: (t, 0, 0, 0)),
        ),
        scratch_shapes=[
            pltpu.VMEM((768, 640), jnp.bfloat16),
            pltpu.VMEM((768, 640), jnp.bfloat16),
            pltpu.VMEM((128, 128), jnp.float32),
            pltpu.VMEM((128, 512), jnp.float32),
            pltpu.VMEM((1, 640), jnp.float32),
        ],
        name="panel_step",
    )(rows, rows, cols, w, nz, noise, X)


def body(features, lengthscale, noise):
    f = jnp.transpose(features, (0, 2, 1)).reshape(4, 2, 24, 128)
    ls = lengthscale.reshape(4, 4, 2, 24).transpose(2, 0, 1, 3).reshape(768)
    w = jnp.broadcast_to((1.0 / (ls * ls))[:, None], (768, 128))
    rows, cols, nz, X = gather(f, noise, w)
    return finish(rows, cols, w, nz, noise, X)


def solution(mesh):
    placed = (P(None, "row", "col"), P(), P(None, "row"))
    return jax.shard_map(
        body,
        mesh=mesh,
        in_specs=placed,
        out_specs=(P(None, "row", None), P(None, "row", None, "col")),
        check_vma=False,
    )
```

```python
import jax
import jax.numpy as jnp
from jax import lax
from jax.experimental import pallas as pl
from jax.experimental.pallas import tpu as pltpu
from jax.sharding import PartitionSpec as P

MESH = pl.DeviceIdType.MESH
NCH = 8


def rcopy(src, dst, ss, rs, dev):
    return pltpu.make_async_remote_copy(
        src_ref=src, dst_ref=dst, send_sem=ss, recv_sem=rs, device_id=dev, device_id_type=MESH
    )


def place():
    r = lax.axis_index("row")
    c = lax.axis_index("col")
    return (
        lax.div(r, 4),
        lax.rem(r, 4),
        lax.div(c, 8),
        lax.rem(lax.div(c, 2), 4),
        lax.rem(c, 2),
    )


def dev(zl, y, x, zh, core):
    return (zl * 4 + y, (x * 4 + zh) * 2 + core)


def comm_kernel(
    f_ref, n_ref, w_ref, rows, cols, nz, X,
    s1s, s1r, loc, s2s, s2r, tcs_, tcr, tts, ttr, cl,
):
    zl, y, x, zh, core = place()
    oc = 1 - core
    zp, zm, zo = lax.rem(zh + 1, 4), lax.rem(zh + 3, 4), lax.rem(zh + 2, 4)
    xp, xm, xo = lax.rem(x + 1, 4), lax.rem(x + 3, 4), lax.rem(x + 2, 4)
    yp, ym = lax.rem(y + 1, 4), lax.rem(y + 3, 4)
    lp, lm = lax.rem(zl + 1, 4), lax.rem(zl + 3, 4)
    d_zp, d_zm = dev(zl, y, x, zp, core), dev(zl, y, x, zm, core)
    d_xp, d_xm = dev(zl, y, xp, zh, core), dev(zl, y, xm, zh, core)
    d_co = dev(zl, y, x, zh, oc)
    d_yp, d_ym = dev(zl, yp, x, zh, core), dev(zl, ym, x, zh, core)
    d_lp, d_lm = dev(lp, y, x, zh, core), dev(lm, y, x, zh, core)
    partners = (d_zp, d_zm, d_xp, d_xm, d_co, d_yp, d_ym, d_lp, d_lm)
    bar = pltpu.get_barrier_semaphore()
    for d in partners:
        pl.semaphore_signal(bar, inc=1, device_id=d, device_id_type=MESH)
    pl.semaphore_wait(bar, len(partners))
    turn = 1 - 2 * core
    y_a = lax.rem(y + turn + 4, 4)
    y_b = lax.rem(y - turn + 4, 4)
    d_a, d_b = dev(zl, y_a, x, zh, core), dev(zl, y_b, x, zh, core)
    sends = []

    def go(cp):
        cp.start()
        sends.append(cp)

    def zrow(zz):
        return pl.multiple_of(((core * 4 + x) * 4 + zz) * 24, 8)

    def xrow(kk, xx):
        return pl.multiple_of((kk * 4 + xx) * 96, 32)

    def zblk(zz, par):
        return rows.at[pl.ds(5 * par, 5 - par), pl.ds(zrow(zz), 24), :]

    def blk(kk, xx, par):
        return rows.at[pl.ds(5 * par, 5 - par), pl.ds(xrow(kk, xx), 96), :]

    def tree(zr, yr, chain):
        on = y == yr
        root = jnp.logical_and(on, zl == zr)
        c_up = jnp.logical_and(on, jnp.logical_and(zl >= zr, zl < 3))
        c_dn = jnp.logical_and(on, jnp.logical_and(zl <= zr, zl > 0))
        c_b = jnp.logical_or(on, y == lax.rem(yr - turn + 4, 4))
        if chain:
            more = y != lax.rem(yr - turn + 4, 4)
            return root, ((c_up, d_lp), (c_dn, d_lm), (more, d_a))
        return root, ((c_up, d_lp), (c_dn, d_lm), (on, d_a), (c_b, d_b))

    def from_root(tr, src, ch, send, recv, k, lsem):
        root, outs = tr

        @pl.when(root)
        def _():
            for i, (cond, d) in enumerate(outs):
                @pl.when(cond)
                def _():
                    rcopy(src, ch, send.at[k, i], recv.at[k], d).start()
            pltpu.make_async_copy(src, ch, lsem.at[k]).start()

    def onward(tr, ch, send, recv, k):
        root, outs = tr

        @pl.when(jnp.logical_not(root))
        def _():
            rcopy(ch, ch, send.at[k, 0], recv.at[k], d_lp).wait_recv()
            for i, (cond, d) in enumerate(outs):
                @pl.when(cond)
                def _():
                    rcopy(ch, ch, send.at[k, i], recv.at[k], d).start()

    def local(tr, src, ch, k, lsem):
        @pl.when(tr[0])
        def _():
            pltpu.make_async_copy(src, ch, lsem.at[k]).wait()

    def done(tr, ch, send, recv, k):
        for i, (cond, d) in enumerate(tr[1]):
            @pl.when(cond)
            def _():
                rcopy(ch, ch, send.at[k, i], recv.at[k], d).wait_send()

    t0 = tree(0, 0, False)
    own4 = rows.at[4, pl.ds(zrow(zh), 24), :]
    first = ((f_ref.at[0, 0], own4), (n_ref, nz))
    for k, (src, ch) in enumerate(first):
        from_root(t0, src, ch, tts, ttr, k, cl.at[0])
    even = rows.at[pl.ds(0, 4), pl.ds(zrow(zh), 24), :]
    me0 = pltpu.make_async_copy(f_ref.at[:, 0], even, loc.at[0])
    me1 = pltpu.make_async_copy(f_ref.at[:, 1], zblk(zh, 1), loc.at[1])
    me0.start()
    me1.start()
    go(rcopy(f_ref.at[:, 1], zblk(zh, 1), s1s.at[0], s1r.at[0], d_zp))
    go(rcopy(f_ref.at[:, 1], zblk(zh, 1), s1s.at[1], s1r.at[1], d_zm))
    for k, (src, ch) in enumerate(first):
        onward(t0, ch, tts, ttr, k)
        local(t0, src, ch, k, cl.at[0])
    me0.wait()
    own = zblk(zh, 0)
    go(rcopy(own, own, s1s.at[2], s1r.at[2], d_zp))
    go(rcopy(own, own, s1s.at[3], s1r.at[3], d_zm))

    def z_in(zz, par, i):
        b = zblk(zz, par)
        rcopy(b, b, s1s.at[i], s1r.at[i], d_zp).wait_recv()
        return b

    b = z_in(zp, 1, 1)
    go(rcopy(b, b, s1s.at[5], s1r.at[5], d_zm))
    b = z_in(zm, 0, 2)
    go(rcopy(b, b, s1s.at[4], s1r.at[4], d_zp))
    z_in(zm, 1, 0)
    z_in(zp, 0, 3)
    z_in(zo, 1, 5)
    me1.wait()

    def own_out(par):
        o = blk(core, x, par)
        for i, d in enumerate((d_xp, d_xm, d_co)):
            go(rcopy(o, o, s2s.at[par, i], s2r.at[par, i], d))

    def x_in(xx, par, i, out):
        b = blk(core, xx, par)
        rcopy(b, b, s2s.at[par, i], s2r.at[par, i], d_xp).wait_recv()
        if i == par:
            go(rcopy(b, b, s2s.at[par, 3], s2r.at[par, 3], (d_xp, d_xm)[par]))
        go(rcopy(b, b, s2s.at[par, out], s2r.at[par, out], d_co))

    def co_in(xx, i):
        for par in range(2):
            b = blk(oc, xx, par)
            rcopy(b, b, s2s.at[par, i], s2r.at[par, i], d_co).wait_recv()

    half = lax.div(x, 2)
    tc = tree(lax.rem(x, 2) * 2 + lax.div(zh, 2), lax.rem(zh, 2) * 2 + core, True)
    order = ((core, x), (oc, x), (core, xm), (core, xp), (oc, xm), (oc, xp), (core, xo), (oc, xo))

    def src_of(k):
        return rows.at[pl.ds(5 * half, 4), pl.ds(xrow(*order[k]), 96), :]

    def dst_of(k):
        return cols.at[:, pl.ds(xrow(*order[k]), 96), :]

    def feed(k):
        from_root(tc, src_of(k), dst_of(k), tcs_, tcr, k, cl.at[1])

    def pass_on(k):
        onward(tc, dst_of(k), tcs_, tcr, k)

    own_out(1)
    z_in(zo, 0, 4)
    own_out(0)
    feed(0)
    for par in (1, 0):
        if par == 0:
            x_in(xm, 0, 0, 4)
            x_in(xp, 0, 1, 5)
        else:
            x_in(xp, 1, 1, 5)
            x_in(xm, 1, 0, 4)
    feed(2)
    feed(3)
    co_in(x, 2)
    feed(1)
    pass_on(0)
    x_in(xo, 1, 3, 6)
    x_in(xo, 0, 3, 6)
    feed(6)
    co_in(xm, 4)
    feed(4)
    co_in(xp, 5)
    feed(5)
    pass_on(2)
    pass_on(3)
    co_in(xo, 6)
    feed(7)
    invert(X, rows.at[4], w_ref, nz[0:1, :])
    eliminate(X, 0, 16)
    for n, k in enumerate((1, 6, 4, 5)):
        pass_on(k)
        eliminate(X, 16 + 12 * n, 12)
    pass_on(7)
    for k in range(NCH):
        local(tc, src_of(k), dst_of(k), k, cl.at[1])
    for k, (src, ch) in enumerate(first):
        done(t0, ch, tts, ttr, k)
    for k in range(NCH):
        done(tc, dst_of(k), tcs_, tcr, k)
    for cp in sends:
        cp.wait_send()


def gather(f, noise, w):
    DMA = pltpu.SemaphoreType.DMA
    vm = pl.BlockSpec(memory_space=pltpu.VMEM)
    return pl.pallas_call(
        comm_kernel,
        out_shape=(
            jax.ShapeDtypeStruct((9, 768, 128), jnp.bfloat16),
            jax.ShapeDtypeStruct((4, 768, 128), jnp.bfloat16),
            jax.ShapeDtypeStruct((8, 128), jnp.float32),
            jax.ShapeDtypeStruct((128, 256), jnp.float32),
        ),
        in_specs=[vm, vm, vm],
        out_specs=(vm, vm, vm, vm),
        scratch_shapes=[
            DMA((6,)), DMA((6,)), DMA((2,)),
            DMA((2, 7)), DMA((2, 7)),
            DMA((NCH, 4)), DMA((NCH,)),
            DMA((2, 4)), DMA((2,)), DMA((2, NCH)),
        ],
        compiler_params=pltpu.CompilerParams(collective_id=0, has_side_effects=True),
        name="gather_features",
    )(f, noise, w)


def invert(X, t_ref, w_ref, n_row):
    T = t_ref[...].astype(jnp.float32)
    Tw = T * w_ref[...]
    tsq = jnp.sum(T * Tw, axis=0, keepdims=True)
    hi = Tw.astype(jnp.bfloat16)
    lo = (Tw - hi.astype(jnp.float32)).astype(jnp.bfloat16)
    g = tdot(t_ref[...], hi) + tdot(t_ref[...], lo)
    tcol = jnp.broadcast_to(tsq, (128, 128)).T
    eye = lax.broadcasted_iota(jnp.int32, (128, 128), 0) == lax.broadcasted_iota(jnp.int32, (128, 128), 1)
    k0 = jnp.exp(g - 0.5 * (tcol + tsq)) + jnp.where(eye, n_row, 0.0)
    X[:, :128] = k0
    X[:, 128:] = jnp.where(eye, 1.0, 0.0)


def tdot(a, b):
    return lax.dot_general(a, b, (((0,), (0,)), ((), ())), preferred_element_type=jnp.float32)


def fdot(a, b):
    return lax.dot_general(
        a, b, (((1,), (0,)), ((), ())), precision=lax.Precision.HIGHEST, preferred_element_type=jnp.float32
    )


def eliminate(X, first, count):
    lane = lax.broadcasted_iota(jnp.int32, (128, 128), 1)
    sub = lax.broadcasted_iota(jnp.int32, (128, 1), 0)

    def at(row, j):
        return jnp.sum(jnp.where(lane[:1] == j, row[:, :128], 0.0), axis=1, keepdims=True)

    def step(i, _):
        j = 2 * i
        S = X[:, :128]
        r0 = X[pl.ds(j, 1), :]
        r1 = X[pl.ds(j + 1, 1), :]
        c0 = jnp.sum(jnp.where(lane == j, S, 0.0), axis=1, keepdims=True)
        c1 = jnp.sum(jnp.where(lane == j + 1, S, 0.0), axis=1, keepdims=True)
        s01 = at(r0, j + 1)
        i0 = 1.0 / at(r0, j)
        a = s01 * i0
        i1 = 1.0 / (at(r1, j + 1) - s01 * a)
        r1 = r1 - a * r0
        f0 = jnp.where(sub > j, c0 * i0, 0.0)
        f1 = jnp.where(sub > j + 1, (c1 - c0 * a) * i1, 0.0)
        X[:, :128] = S - f0 * r0[:, :128] - f1 * r1[:, :128]
        X[:, 128:] = X[:, 128:] - f0 * r0[:, 128:] - f1 * r1[:, 128:]
        return 0

    lax.fori_loop(first, first + count, step, 0)


def scaled_inverse(X):
    lane = lax.broadcasted_iota(jnp.int32, (128, 128), 1)
    sub = lax.broadcasted_iota(jnp.int32, (128, 128), 0)
    d = jnp.sum(jnp.where(lane == sub, X[:, :128], 0.0), axis=1, keepdims=True)
    return X[:, 128:] * lax.rsqrt(d)


def slot(t):
    return 5 * (t % 2) + t // 2


def main_kernel(rows, cols, w_ref, nz, n_ref, X, pan, out, whi, wlo):
    r = lax.axis_index("row")
    c = lax.axis_index("col")
    t0 = rows.at[4]
    inv = scaled_inverse(X)
    inv_t = inv.T
    eye = lax.broadcasted_iota(jnp.int32, (128, 128), 0) == lax.broadcasted_iota(jnp.int32, (128, 128), 1)
    w = w_ref[...]

    def split(x, at):
        hi = x.astype(jnp.bfloat16)
        whi[:, at * 128:(at + 1) * 128] = hi
        wlo[:, at * 128:(at + 1) * 128] = (x - hi.astype(jnp.float32)).astype(jnp.bfloat16)

    T = t0[...].astype(jnp.float32)
    Tw = T * w
    split(Tw, 4)
    tsq = jnp.sum(T * Tw, axis=0, keepdims=True)
    tcol = jnp.broadcast_to(tsq, (128, 128)).T
    csq = []
    pct = []
    for u in range(4):
        C = cols[u].astype(jnp.float32)
        Cw = C * w
        split(Cw, u)
        cs = jnp.sum(C * Cw, axis=0, keepdims=True)
        csq.append(cs)
        g = tdot(whi[:, 512:], cols[u]) + tdot(wlo[:, 512:], cols[u])
        kc = jnp.exp(g - 0.5 * (tcol + cs))
        kc = kc + jnp.where(jnp.logical_and(eye, u * 32 + c == 0), nz[0:1, :], 0.0)
        pct.append(fdot(inv, kc))
    sq = jnp.concatenate(csq + [tsq], axis=1)
    pt = jnp.concatenate(pct, axis=1)
    for t in range(8):
        a = rows[slot(t)]
        af = a.astype(jnp.float32)
        asq = jnp.sum(af * af * w, axis=0, keepdims=True)
        acol = jnp.broadcast_to(asq, (128, 128)).T[:, :1]
        g = tdot(a, whi[...]) + tdot(a, wlo[...])
        k = jnp.exp(g - 0.5 * (acol + sq))
        nr = jnp.where(eye, n_ref[t:t + 1, :], 0.0)
        ka = k[:, 512:] + jnp.where(t * 16 + r == 0, nr, 0.0)
        p = fdot(ka, inv_t)
        pan[t] = p
        for u in range(4):
            x = k[:, u * 128:(u + 1) * 128] + jnp.where(t * 16 + r == u * 32 + c, nr, 0.0)
            out[t, :, u, :] = x - fdot(p, pt[:, u * 128:(u + 1) * 128])


def finish(rows, cols, w, nz, noise, X):
    vm = pl.BlockSpec(memory_space=pltpu.VMEM)
    return pl.pallas_call(
        main_kernel,
        out_shape=(
            jax.ShapeDtypeStruct((8, 128, 128), jnp.float32),
            jax.ShapeDtypeStruct((8, 128, 4, 128), jnp.float32),
        ),
        in_specs=[vm] * 6,
        out_specs=(vm, vm),
        scratch_shapes=[
            pltpu.VMEM((768, 640), jnp.bfloat16),
            pltpu.VMEM((768, 640), jnp.bfloat16),
        ],
        name="panel_step",
    )(rows, cols, w, nz, noise, X)


def body(features, lengthscale, noise):
    f = jnp.transpose(features, (0, 2, 1)).reshape(4, 2, 24, 128)
    ls = lengthscale.reshape(4, 4, 2, 24).transpose(2, 0, 1, 3).reshape(768)
    w = jnp.broadcast_to((1.0 / (ls * ls))[:, None], (768, 128))
    rows, cols, nz, X = gather(f, noise, w)
    return finish(rows, cols, w, nz, noise, X)


def solution(mesh):
    placed = (P(None, "row", "col"), P(), P(None, "row"))
    return jax.shard_map(
        body,
        mesh=mesh,
        in_specs=placed,
        out_specs=(P(None, "row", None), P(None, "row", None, "col")),
        check_vma=False,
    )
```

```python
import jax
import jax.numpy as jnp
from jax import lax
from jax.experimental import pallas as pl
from jax.experimental.pallas import tpu as pltpu
from jax.sharding import PartitionSpec as P

MESH = pl.DeviceIdType.MESH
NCH = 16


def rcopy(src, dst, ss, rs, dev):
    return pltpu.make_async_remote_copy(
        src_ref=src, dst_ref=dst, send_sem=ss, recv_sem=rs, device_id=dev, device_id_type=MESH
    )


def place():
    r = lax.axis_index("row")
    c = lax.axis_index("col")
    return (
        lax.div(r, 4),
        lax.rem(r, 4),
        lax.div(c, 8),
        lax.rem(lax.div(c, 2), 4),
        lax.rem(c, 2),
    )


def dev(zl, y, x, zh, core):
    return (zl * 4 + y, (x * 4 + zh) * 2 + core)


def comm_kernel(
    f_ref, n_ref, w_ref, rows, cols, nz, X,
    s1s, s1r, loc, s2s, s2r, tcs_, tcr, tts, ttr, cl,
):
    zl, y, x, zh, core = place()
    oc = 1 - core
    zp, zm, zo = lax.rem(zh + 1, 4), lax.rem(zh + 3, 4), lax.rem(zh + 2, 4)
    xp, xm, xo = lax.rem(x + 1, 4), lax.rem(x + 3, 4), lax.rem(x + 2, 4)
    yp, ym = lax.rem(y + 1, 4), lax.rem(y + 3, 4)
    lp, lm = lax.rem(zl + 1, 4), lax.rem(zl + 3, 4)
    d_zp, d_zm = dev(zl, y, x, zp, core), dev(zl, y, x, zm, core)
    d_xp, d_xm = dev(zl, y, xp, zh, core), dev(zl, y, xm, zh, core)
    d_co = dev(zl, y, x, zh, oc)
    d_yp, d_ym = dev(zl, yp, x, zh, core), dev(zl, ym, x, zh, core)
    d_lp, d_lm = dev(lp, y, x, zh, core), dev(lm, y, x, zh, core)
    partners = (d_zp, d_zm, d_xp, d_xm, d_co, d_yp, d_ym, d_lp, d_lm)
    bar = pltpu.get_barrier_semaphore()
    for d in partners:
        pl.semaphore_signal(bar, inc=1, device_id=d, device_id_type=MESH)
    pl.semaphore_wait(bar, len(partners))
    turn = 1 - 2 * core
    y_a = lax.rem(y + turn + 4, 4)
    y_b = lax.rem(y - turn + 4, 4)
    d_a, d_b = dev(zl, y_a, x, zh, core), dev(zl, y_b, x, zh, core)
    sends = []

    def go(cp):
        cp.start()
        sends.append(cp)

    def zrow(zz):
        return pl.multiple_of(((core * 4 + x) * 4 + zz) * 24, 8)

    def xrow(kk, xx):
        return pl.multiple_of((kk * 4 + xx) * 96, 32)

    def zblk(zz, par):
        return rows.at[pl.ds(5 * par, 5 - par), pl.ds(zrow(zz), 24), :]

    def blk(kk, xx, par):
        return rows.at[pl.ds(5 * par, 5 - par), pl.ds(xrow(kk, xx), 96), :]

    def tree(zr, yr):
        on = y == yr
        root = jnp.logical_and(on, zl == zr)
        c_up = jnp.logical_and(on, jnp.logical_and(zl >= zr, zl < 3))
        c_dn = jnp.logical_and(on, jnp.logical_and(zl <= zr, zl > 0))
        c_b = jnp.logical_or(on, y == lax.rem(yr - turn + 4, 4))
        return root, ((c_up, d_lp), (c_dn, d_lm), (on, d_a), (c_b, d_b))

    def from_root(tr, src, ch, send, recv, k, lsem):
        root, outs = tr

        @pl.when(root)
        def _():
            for i, (cond, d) in enumerate(outs):
                @pl.when(cond)
                def _():
                    rcopy(src, ch, send.at[k, i], recv.at[k], d).start()
            pltpu.make_async_copy(src, ch, lsem.at[k]).start()

    def onward(tr, ch, send, recv, k):
        root, outs = tr

        @pl.when(jnp.logical_not(root))
        def _():
            rcopy(ch, ch, send.at[k, 0], recv.at[k], d_lp).wait_recv()
            for i, (cond, d) in enumerate(outs):
                @pl.when(cond)
                def _():
                    rcopy(ch, ch, send.at[k, i], recv.at[k], d).start()

    def local(tr, src, ch, k, lsem):
        @pl.when(tr[0])
        def _():
            pltpu.make_async_copy(src, ch, lsem.at[k]).wait()

    def done(tr, ch, send, recv, k):
        for i, (cond, d) in enumerate(tr[1]):
            @pl.when(cond)
            def _():
                rcopy(ch, ch, send.at[k, i], recv.at[k], d).wait_send()

    t0 = tree(0, 0)
    own4 = rows.at[4, pl.ds(zrow(zh), 24), :]
    first = ((f_ref.at[0, 0], own4), (n_ref, nz))
    for k, (src, ch) in enumerate(first):
        from_root(t0, src, ch, tts, ttr, k, cl.at[0])
    even = rows.at[pl.ds(0, 4), pl.ds(zrow(zh), 24), :]
    me0 = pltpu.make_async_copy(f_ref.at[:, 0], even, loc.at[0])
    me1 = pltpu.make_async_copy(f_ref.at[:, 1], zblk(zh, 1), loc.at[1])
    me0.start()
    me1.start()
    go(rcopy(f_ref.at[:, 1], zblk(zh, 1), s1s.at[0], s1r.at[0], d_zp))
    go(rcopy(f_ref.at[:, 1], zblk(zh, 1), s1s.at[1], s1r.at[1], d_zm))
    for k, (src, ch) in enumerate(first):
        onward(t0, ch, tts, ttr, k)
        local(t0, src, ch, k, cl.at[0])
    me0.wait()
    own = zblk(zh, 0)
    go(rcopy(own, own, s1s.at[2], s1r.at[2], d_zp))
    go(rcopy(own, own, s1s.at[3], s1r.at[3], d_zm))

    def z_in(zz, par, i):
        b = zblk(zz, par)
        rcopy(b, b, s1s.at[i], s1r.at[i], d_zp).wait_recv()
        return b

    b = z_in(zp, 1, 1)
    go(rcopy(b, b, s1s.at[5], s1r.at[5], d_zm))
    b = z_in(zm, 0, 2)
    go(rcopy(b, b, s1s.at[4], s1r.at[4], d_zp))
    z_in(zm, 1, 0)
    z_in(zp, 0, 3)
    z_in(zo, 1, 5)
    me1.wait()

    def own_out(par):
        o = blk(core, x, par)
        for i, d in enumerate((d_xp, d_xm, d_co)):
            go(rcopy(o, o, s2s.at[par, i], s2r.at[par, i], d))

    def x_in(xx, par, i, out):
        b = blk(core, xx, par)
        rcopy(b, b, s2s.at[par, i], s2r.at[par, i], d_xp).wait_recv()
        if i == par:
            go(rcopy(b, b, s2s.at[par, 3], s2r.at[par, 3], (d_xp, d_xm)[par]))
        go(rcopy(b, b, s2s.at[par, out], s2r.at[par, out], d_co))

    def co_in(xx, i):
        for par in range(2):
            b = blk(oc, xx, par)
            rcopy(b, b, s2s.at[par, i], s2r.at[par, i], d_co).wait_recv()

    half = lax.div(x, 2)
    tc = tree(lax.rem(x, 2) * 2 + lax.div(zh, 2), lax.rem(zh, 2) * 2 + core)
    order = ((core, x), (oc, x), (core, xm), (core, xp), (oc, xm), (oc, xp), (core, xo), (oc, xo))

    def src_of(k):
        return rows.at[pl.ds(5 * half + 2 * (k % 2), 2), pl.ds(xrow(*order[k // 2]), 96), :]

    def dst_of(k):
        return cols.at[pl.ds(2 * (k % 2), 2), pl.ds(xrow(*order[k // 2]), 96), :]

    def feed(k):
        for n in (2 * k, 2 * k + 1):
            from_root(tc, src_of(n), dst_of(n), tcs_, tcr, n, cl.at[1])

    def pass_half(n):
        onward(tc, dst_of(n), tcs_, tcr, n)

    def pass_on(k):
        pass_half(2 * k)
        pass_half(2 * k + 1)

    own_out(1)
    z_in(zo, 0, 4)
    own_out(0)
    feed(0)
    for par in (1, 0):
        if par == 0:
            x_in(xm, 0, 0, 4)
            x_in(xp, 0, 1, 5)
        else:
            x_in(xp, 1, 1, 5)
            x_in(xm, 1, 0, 4)
    feed(2)
    feed(3)
    co_in(x, 2)
    feed(1)
    pass_on(0)
    x_in(xo, 1, 3, 6)
    x_in(xo, 0, 3, 6)
    feed(6)
    co_in(xm, 4)
    feed(4)
    co_in(xp, 5)
    feed(5)
    pass_on(2)
    pass_on(3)
    co_in(xo, 6)
    feed(7)
    invert(X, rows.at[4], w_ref, nz[0:1, :])
    eliminate(X, 0, 16)
    for n, k in enumerate((1, 6, 4, 5)):
        pass_half(2 * k)
        eliminate(X, 16 + 12 * n, 6)
        pass_half(2 * k + 1)
        eliminate(X, 22 + 12 * n, 6)
    pass_on(7)
    for k in range(NCH):
        local(tc, src_of(k), dst_of(k), k, cl.at[1])
    for k, (src, ch) in enumerate(first):
        done(t0, ch, tts, ttr, k)
    for k in range(NCH):
        done(tc, dst_of(k), tcs_, tcr, k)
    for cp in sends:
        cp.wait_send()


def gather(f, noise, w):
    DMA = pltpu.SemaphoreType.DMA
    vm = pl.BlockSpec(memory_space=pltpu.VMEM)
    return pl.pallas_call(
        comm_kernel,
        out_shape=(
            jax.ShapeDtypeStruct((9, 768, 128), jnp.bfloat16),
            jax.ShapeDtypeStruct((4, 768, 128), jnp.bfloat16),
            jax.ShapeDtypeStruct((8, 128), jnp.float32),
            jax.ShapeDtypeStruct((128, 256), jnp.float32),
        ),
        in_specs=[vm, vm, vm],
        out_specs=(vm, vm, vm, vm),
        scratch_shapes=[
            DMA((6,)), DMA((6,)), DMA((2,)),
            DMA((2, 7)), DMA((2, 7)),
            DMA((NCH, 4)), DMA((NCH,)),
            DMA((2, 4)), DMA((2,)), DMA((2, NCH)),
        ],
        compiler_params=pltpu.CompilerParams(collective_id=0, has_side_effects=True),
        name="gather_features",
    )(f, noise, w)


def invert(X, t_ref, w_ref, n_row):
    T = t_ref[...].astype(jnp.float32)
    Tw = T * w_ref[...]
    tsq = jnp.sum(T * Tw, axis=0, keepdims=True)
    hi = Tw.astype(jnp.bfloat16)
    lo = (Tw - hi.astype(jnp.float32)).astype(jnp.bfloat16)
    g = tdot(t_ref[...], hi) + tdot(t_ref[...], lo)
    tcol = jnp.broadcast_to(tsq, (128, 128)).T
    eye = lax.broadcasted_iota(jnp.int32, (128, 128), 0) == lax.broadcasted_iota(jnp.int32, (128, 128), 1)
    k0 = jnp.exp(g - 0.5 * (tcol + tsq)) + jnp.where(eye, n_row, 0.0)
    X[:, :128] = k0
    X[:, 128:] = jnp.where(eye, 1.0, 0.0)


def tdot(a, b):
    return lax.dot_general(a, b, (((0,), (0,)), ((), ())), preferred_element_type=jnp.float32)


def fdot(a, b):
    return lax.dot_general(
        a, b, (((1,), (0,)), ((), ())), precision=lax.Precision.HIGHEST, preferred_element_type=jnp.float32
    )


def eliminate(X, first, count):
    lane = lax.broadcasted_iota(jnp.int32, (128, 128), 1)
    sub = lax.broadcasted_iota(jnp.int32, (128, 1), 0)

    def at(row, j):
        return jnp.sum(jnp.where(lane[:1] == j, row[:, :128], 0.0), axis=1, keepdims=True)

    def step(i, _):
        j = 2 * i
        S = X[:, :128]
        r0 = X[pl.ds(j, 1), :]
        r1 = X[pl.ds(j + 1, 1), :]
        c0 = jnp.sum(jnp.where(lane == j, S, 0.0), axis=1, keepdims=True)
        c1 = jnp.sum(jnp.where(lane == j + 1, S, 0.0), axis=1, keepdims=True)
        s01 = at(r0, j + 1)
        i0 = 1.0 / at(r0, j)
        a = s01 * i0
        i1 = 1.0 / (at(r1, j + 1) - s01 * a)
        r1 = r1 - a * r0
        f0 = jnp.where(sub > j, c0 * i0, 0.0)
        f1 = jnp.where(sub > j + 1, (c1 - c0 * a) * i1, 0.0)
        X[:, :128] = S - f0 * r0[:, :128] - f1 * r1[:, :128]
        X[:, 128:] = X[:, 128:] - f0 * r0[:, 128:] - f1 * r1[:, 128:]
        return 0

    lax.fori_loop(first, first + count, step, 0)


def scaled_inverse(X):
    lane = lax.broadcasted_iota(jnp.int32, (128, 128), 1)
    sub = lax.broadcasted_iota(jnp.int32, (128, 128), 0)
    d = jnp.sum(jnp.where(lane == sub, X[:, :128], 0.0), axis=1, keepdims=True)
    return X[:, 128:] * lax.rsqrt(d)


def slot(t):
    return 5 * (t % 2) + t // 2


def main_kernel(rows, cols, w_ref, nz, n_ref, X, pan, out, whi, wlo):
    r = lax.axis_index("row")
    c = lax.axis_index("col")
    t0 = rows.at[4]
    inv = scaled_inverse(X)
    inv_t = inv.T
    eye = lax.broadcasted_iota(jnp.int32, (128, 128), 0) == lax.broadcasted_iota(jnp.int32, (128, 128), 1)
    w = w_ref[...]

    def split(x, at):
        hi = x.astype(jnp.bfloat16)
        whi[:, at * 128:(at + 1) * 128] = hi
        wlo[:, at * 128:(at + 1) * 128] = (x - hi.astype(jnp.float32)).astype(jnp.bfloat16)

    T = t0[...].astype(jnp.float32)
    Tw = T * w
    split(Tw, 4)
    tsq = jnp.sum(T * Tw, axis=0, keepdims=True)
    tcol = jnp.broadcast_to(tsq, (128, 128)).T
    csq = []
    pct = []
    for u in range(4):
        C = cols[u].astype(jnp.float32)
        Cw = C * w
        split(Cw, u)
        cs = jnp.sum(C * Cw, axis=0, keepdims=True)
        csq.append(cs)
        g = tdot(whi[:, 512:], cols[u]) + tdot(wlo[:, 512:], cols[u])
        kc = jnp.exp(g - 0.5 * (tcol + cs))
        kc = kc + jnp.where(jnp.logical_and(eye, u * 32 + c == 0), nz[0:1, :], 0.0)
        pct.append(fdot(inv, kc))
    sq = jnp.concatenate(csq + [tsq], axis=1)
    pt = jnp.concatenate(pct, axis=1)
    for t in range(8):
        a = rows[slot(t)]
        af = a.astype(jnp.float32)
        asq = jnp.sum(af * af * w, axis=0, keepdims=True)
        acol = jnp.broadcast_to(asq, (128, 128)).T[:, :1]
        g = tdot(a, whi[...]) + tdot(a, wlo[...])
        k = jnp.exp(g - 0.5 * (acol + sq))
        nr = jnp.where(eye, n_ref[t:t + 1, :], 0.0)
        ka = k[:, 512:] + jnp.where(t * 16 + r == 0, nr, 0.0)
        p = fdot(ka, inv_t)
        pan[t] = p
        for u in range(4):
            x = k[:, u * 128:(u + 1) * 128] + jnp.where(t * 16 + r == u * 32 + c, nr, 0.0)
            out[t, :, u, :] = x - fdot(p, pt[:, u * 128:(u + 1) * 128])


def finish(rows, cols, w, nz, noise, X):
    vm = pl.BlockSpec(memory_space=pltpu.VMEM)
    return pl.pallas_call(
        main_kernel,
        out_shape=(
            jax.ShapeDtypeStruct((8, 128, 128), jnp.float32),
            jax.ShapeDtypeStruct((8, 128, 4, 128), jnp.float32),
        ),
        in_specs=[vm] * 6,
        out_specs=(vm, vm),
        scratch_shapes=[
            pltpu.VMEM((768, 640), jnp.bfloat16),
            pltpu.VMEM((768, 640), jnp.bfloat16),
        ],
        name="panel_step",
    )(rows, cols, w, nz, noise, X)


def body(features, lengthscale, noise):
    f = jnp.transpose(features, (0, 2, 1)).reshape(4, 2, 24, 128)
    ls = lengthscale.reshape(4, 4, 2, 24).transpose(2, 0, 1, 3).reshape(768)
    w = jnp.broadcast_to((1.0 / (ls * ls))[:, None], (768, 128))
    rows, cols, nz, X = gather(f, noise, w)
    return finish(rows, cols, w, nz, noise, X)


def solution(mesh):
    placed = (P(None, "row", "col"), P(), P(None, "row"))
    return jax.shard_map(
        body,
        mesh=mesh,
        in_specs=placed,
        out_specs=(P(None, "row", None), P(None, "row", None, "col")),
        check_vma=False,
    )
```
